32 devices in a mesh: dp: 16 (over z, x, core), expert: 2 (over y).
Axes of the slice: x: 2, y: 2, z: 4, core: 2. Of those that a mesh axis runs over, the one named last changes fastest.
Arguments:
- stash: bfloat16 [4096, 6144], P(('dp', 'expert')), may hold values from -6 to 6
- scales: bfloat16 [4096, 48], P(('dp', 'expert')), may hold values from 0.099609375 to 2
- out_grad: bfloat16 [4096, 6144], P(('dp', 'expert')), may hold values from -6 to 6
- route_ids: int32 [4096, 2], P(('dp', 'expert')), may hold values from 0 to 1, as said below
- gates: float32 [4096, 2], P(('dp', 'expert')), may hold values from 0.1 to 1
- w_gate_up: bfloat16 [2, 6144, 512], P('expert'), may hold values from -0.15625 to 0.15625
- w_down: bfloat16 [2, 6144, 256], P('expert', 'dp'), may hold values from -0.078125 to 0.078125
Outputs:
- input_grad: bfloat16 [4096, 6144], P(('dp', 'expert'))
- grad_gate_up: float32 [2, 6144, 512], P('expert', 'dp')
The draws below stay inside these ranges and needn't reach their ends.
Inputs may be any that keep to these rules, and one draw needn't show every extreme that they name: `route_ids`: each token names two different experts. Within each aligned block of 128 tokens no expert is named more than 128 times. In every run of 2 aligned blocks that starts at a multiple of 2 blocks, some expert is named exactly 128 times in each block of the run.
All inputs are finite; a program needn't handle non-finite values.
Results may differ from the reference program's by a relative error of at most 0.023.
Values may be sent and summed in bfloat16 or wider, within the bound.
No kernel may reach another device: no remote copies, remote signals or barrier semaphores. Data moves between devices by JAX's collectives and lax.ppermute only.
A program may use at most 128 MiB of HBM per device.

```python
import math
import jax
import jax.numpy as jnp
from jax import lax

D = 6144
HID = 256
QBLK = 128
TOK_DEV = 128
EXPERTS = 2
CAP = 128
TOKENS = 4096
N_DP = 16
N_EXPERT = 2


def device_routes(device_key, hot_expert):
    key_second, key_count, key_perm, key_flip = jax.random.split(device_key, 4)
    slot_total = 2 * TOK_DEV
    second_expert = (hot_expert + jax.random.randint(key_second, (), 1, EXPERTS)) % EXPERTS
    lowest = max(0, slot_total - CAP - (EXPERTS - 2) * CAP)
    highest = min(CAP, slot_total - CAP)
    second_count = jax.random.randint(key_count, (), lowest, highest + 1)
    offsets = jnp.arange(1, EXPERTS, dtype=jnp.int32)
    candidates = (hot_expert + offsets) % EXPERTS
    order_key = jnp.where(candidates == second_expert, EXPERTS, 0) + offsets
    others = candidates[jnp.argsort(order_key)]
    spread = max(EXPERTS - 2, 1)
    places = jnp.arange(slot_total, dtype=jnp.int32)
    rest_index = jnp.maximum(places - CAP - second_count, 0) % spread
    labels = jnp.where(places < CAP, hot_expert, jnp.where(places < CAP + second_count, second_expert, others[rest_index]))
    labels = jnp.sort(labels)
    paired = jnp.stack([labels[:TOK_DEV], labels[TOK_DEV:]], axis=1)
    paired = paired[jax.random.permutation(key_perm, TOK_DEV)]
    flipped = jax.random.randint(key_flip, (TOK_DEV, 1), 0, 2)
    paired = jnp.where(flipped == 1, paired[:, ::-1], paired)
    return paired.astype(jnp.int32)


def draw_route_ids(key, part):
    base_key = jax.random.fold_in(key, 7)
    key_hot, key_devices = jax.random.split(base_key)
    hot_rows = jax.random.randint(key_hot, (N_DP,), 0, EXPERTS)
    hot_devices = jnp.repeat(hot_rows, N_EXPERT)
    device_keys = jax.random.split(key_devices, N_DP * N_EXPERT)
    paired = jax.vmap(device_routes)(device_keys, hot_devices)
    return paired.reshape(TOKENS, 2).astype(jnp.int32)


def with_spikes(result, own_key, source, target, blocks, factor):
    owner, partner = [(jnp.arange(result.shape[dim]) // (result.shape[dim] // blocks)).reshape([-1 if axis == dim else 1 for axis in range(result.ndim)]) for dim in (source, target)]
    chosen = jax.random.permutation(own_key, blocks)[partner]
    strong = (owner == chosen) | (owner == (partner + blocks // 2) % blocks)
    return jnp.where(strong, factor * result, result)


def block_scale(stream_key, shape, pieces, low, largest):
    level = 1.0
    for position, blocks in pieces:
        steps = jax.random.uniform(jax.random.fold_in(jax.random.fold_in(stream_key, 6), position), (blocks,), jnp.float32, low / len(pieces), largest / len(pieces))
        level = level * jnp.repeat(jnp.exp(steps), shape[position] // blocks).reshape((-1,) + (1,) * (len(shape) - 1 - position))
    return level


def noise(key, shape, scale, bound, pieces=(), kind=jnp.bfloat16):
    result = jax.random.normal(key, shape, jnp.float32) * scale
    if len(pieces) > 0:
        result = block_scale(key, shape, pieces, -0.22, 0.18) * result
    return jnp.clip(result, min=-bound, max=bound).astype(kind)


def noise_with(own_key, shape, width, reach, cuts, heavy, held_as=jnp.bfloat16):
    entries = width * jax.random.normal(own_key, shape, jnp.float32)
    if cuts:
        entries = entries * block_scale(own_key, shape, cuts, -0.22, 0.18)
    return jnp.clip(with_spikes(entries, jax.random.fold_in(own_key, 3), *heavy), -reach, reach).astype(held_as)


def setup_inputs(seed: int = 0) -> dict:
    arg_keys = jax.random.split(jax.random.key(seed), 8)
    stash = noise_with(arg_keys[0], (TOKENS, D), 1.0, 6.0, ((0, 32),), (0, 1, 32, 2.75))
    scales = jnp.clip(jnp.exp(math.log(2.0) - 2.9996462 * jax.random.uniform(arg_keys[1], (TOKENS, D // QBLK), jnp.float32) ** block_scale(arg_keys[1], (TOKENS, D // QBLK), ((0, 32),), -0.2, 0.2)), 0.099609375, 2.0).astype(jnp.bfloat16)
    out_grad = noise(arg_keys[2], (TOKENS, D), 1.0, 6.0, ((0, 32),))
    route_ids = draw_route_ids(jax.random.fold_in(arg_keys[7], 71), 0)
    gates = jnp.clip(0.1 + 0.9 * jax.random.uniform(arg_keys[4], (TOKENS, 2), jnp.float32) ** block_scale(arg_keys[4], (TOKENS, 2), ((0, 32),), -0.2, 0.2), 0.1, 1.0)
    w_gate_up = noise(arg_keys[5], (EXPERTS, D, 2 * HID), (D // 4) ** -0.5, 0.15625, ((0, 2),))
    w_down = noise(arg_keys[6], (EXPERTS, D, HID), D ** -0.5, 0.078125, ((0, 2), (1, 16)))
    return {"stash": stash, "scales": scales, "out_grad": out_grad, "route_ids": route_ids, "gates": gates, "w_gate_up": w_gate_up, "w_down": w_down}


def dispatch_plan(route_ids):
    flat_ids = route_ids.reshape(-1).astype(jnp.int32)
    onehot = (flat_ids[:, None] == jnp.arange(EXPERTS, dtype=jnp.int32)[None, :]).astype(jnp.int32)
    earlier = (jnp.cumsum(onehot, axis=0) - onehot).astype(jnp.int32)
    ranking = jnp.sum(earlier * onehot, axis=1).astype(jnp.int32)
    destination = (flat_ids * CAP + ranking).astype(jnp.int32)
    slot_total = 2 * TOK_DEV
    source = jnp.full((EXPERTS * CAP,), slot_total, jnp.int32)
    source = source.at[destination].set(jnp.arange(slot_total, dtype=jnp.int32))
    return destination, source


def source_side(stash, scales, out_grad, route_ids, gates):
    destination, source = dispatch_plan(route_ids)
    slot_total = 2 * TOK_DEV
    live_rows = (source < slot_total)[:, None]
    token_index = jnp.minimum(source // 2, TOK_DEV - 1).astype(jnp.int32)
    slot_index = jnp.minimum(source, slot_total - 1).astype(jnp.int32)
    sent_stash = jnp.where(live_rows, stash[token_index], jnp.zeros((), stash.dtype))
    sent_scale = jnp.where(live_rows, scales[token_index], jnp.zeros((), scales.dtype))
    weighted = gates.reshape(-1)[slot_index][:, None] * out_grad[token_index].astype(jnp.float32)
    sent_grad = jnp.where(live_rows, weighted, jnp.zeros((), jnp.float32)).astype(jnp.bfloat16)
    return (sent_stash.reshape(EXPERTS, CAP, D), sent_scale.reshape(EXPERTS, CAP, D // QBLK),
            sent_grad.reshape(EXPERTS, CAP, D), destination)


def dequantize(stash_rows, scale_rows):
    row_total = stash_rows.shape[0]
    blocks = scale_rows.shape[1]
    scaled = stash_rows.reshape(row_total, blocks, -1).astype(jnp.float32) * scale_rows.astype(jnp.float32)[:, :, None]
    return scaled.reshape(row_total, -1).astype(jnp.bfloat16)


def gated_backward(gate_up, back_hidden):
    hidden = back_hidden.shape[1]
    gate_value = gate_up[:, :hidden]
    up_value = gate_up[:, hidden:]
    sigmoid_gate = jax.nn.sigmoid(gate_value)
    grad_gate = back_hidden * up_value * sigmoid_gate * (1.0 + gate_value * (1.0 - sigmoid_gate))
    grad_up = back_hidden * gate_value * sigmoid_gate
    return jnp.concatenate([grad_gate, grad_up], axis=1).astype(jnp.bfloat16)


def expert_pass(inputs):
    got_stash, got_scale, got_grad, weight_in, weight_out = inputs
    row_total = got_stash.shape[0] * got_stash.shape[1]
    features = dequantize(got_stash.reshape(row_total, D), got_scale.reshape(row_total, -1))
    gate_up = jnp.dot(features, weight_in, preferred_element_type=jnp.float32)
    upstream = got_grad.reshape(row_total, D)
    back_hidden = jnp.dot(upstream, weight_out, preferred_element_type=jnp.float32)
    hidden_grad = gated_backward(gate_up, back_hidden)
    slot_grads = lax.dot_general(hidden_grad, weight_in, (((1,), (1,)), ((), ())),
                                 preferred_element_type=jnp.float32).astype(jnp.bfloat16)
    partial_grad = lax.dot_general(features, hidden_grad, (((0,), (0,)), ((), ())),
                                   preferred_element_type=jnp.float32)
    return slot_grads, partial_grad


def combine_slots(returned, destination):
    picked = returned[destination].astype(jnp.float32).reshape(TOK_DEV, 2, D)
    return jnp.sum(picked, axis=1).astype(jnp.bfloat16)


def reference(stash, scales, out_grad, route_ids, gates, w_gate_up, w_down):
    blocks = D // QBLK
    stacked = (stash.reshape(N_DP, N_EXPERT, TOK_DEV, D),
               scales.reshape(N_DP, N_EXPERT, TOK_DEV, blocks),
               out_grad.reshape(N_DP, N_EXPERT, TOK_DEV, D),
               route_ids.reshape(N_DP, N_EXPERT, TOK_DEV, 2),
               gates.reshape(N_DP, N_EXPERT, TOK_DEV, 2))

    def row_step(running, row_inputs):
        row_stash, row_scales, row_grad, row_ids, row_gates = row_inputs
        sent_stash, sent_scale, sent_grad, destination = jax.vmap(source_side)(
            row_stash, row_scales, row_grad, row_ids, row_gates)
        received = (jnp.swapaxes(sent_stash, 0, 1), jnp.swapaxes(sent_scale, 0, 1),
                    jnp.swapaxes(sent_grad, 0, 1), w_gate_up, w_down)
        slot_grads, partial_grad = lax.map(expert_pass, received)
        returned = jnp.swapaxes(slot_grads.reshape(EXPERTS, N_EXPERT, CAP, D), 0, 1)
        returned = returned.reshape(N_EXPERT, EXPERTS * CAP, D)
        token_grads = jax.vmap(combine_slots)(returned, destination)
        return running + partial_grad, token_grads

    initial = jnp.zeros((EXPERTS, D, 2 * HID), jnp.float32)
    total_grad, token_grads = lax.scan(row_step, initial, stacked)
    return token_grads.reshape(TOKENS, D), total_grad / N_DP
```

```python
import functools
import math

import jax
import jax.numpy as jnp
from jax import lax
from jax.experimental import pallas as pl
from jax.experimental.pallas import tpu as pltpu
from jax.sharding import PartitionSpec as P


def dispatch_plan(route_ids, experts, capacity, tokens):
    flat_ids = route_ids.reshape(-1)
    onehot = (flat_ids[:, None] == jnp.arange(experts, dtype=jnp.int32)[None, :]).astype(jnp.int32)
    earlier = jnp.cumsum(onehot, axis=0) - onehot
    ranking = jnp.sum(earlier * onehot, axis=1)
    destination = flat_ids * capacity + ranking
    slot_total = 2 * tokens
    source = jnp.full((experts * capacity,), slot_total, jnp.int32)
    source = source.at[destination].set(jnp.arange(slot_total, dtype=jnp.int32))
    return (destination, source)


def dequantize(stash_rows, scale_rows):
    row_total = stash_rows.shape[0]
    blocks = scale_rows.shape[1]
    scaled = (
        stash_rows.reshape(row_total, blocks, -1).astype(jnp.float32)
        * scale_rows.astype(jnp.float32)[:, :, None]
    )
    return scaled.reshape(row_total, -1).astype(jnp.bfloat16)


def gated_backward(gate_up, back_hidden):
    hidden = back_hidden.shape[1]
    gate_value = gate_up[:, :hidden]
    up_value = gate_up[:, hidden:]
    sigmoid_gate = jax.nn.sigmoid(gate_value)
    grad_gate = back_hidden * up_value * sigmoid_gate * (1.0 + gate_value * (1.0 - sigmoid_gate))
    grad_up = back_hidden * gate_value * sigmoid_gate
    return jnp.concatenate([grad_gate, grad_up], axis=1).astype(jnp.bfloat16)


def on_device(stash, scales, out_grad, route_ids, gates, w_gate_up, w_down):
    tokens, feature_width = stash.shape
    blocks = scales.shape[1]
    hidden = w_down.shape[2]
    experts = lax.axis_size("expert")
    dp_count = lax.axis_size("dp")
    capacity = min(tokens, 7 * tokens // (2 * experts))
    row_total = experts * capacity
    destination, source = dispatch_plan(route_ids, experts, capacity, tokens)
    slot_total = 2 * tokens
    live_rows = (source < slot_total)[:, None]
    token_index = jnp.minimum(source // 2, tokens - 1)
    slot_index = jnp.minimum(source, slot_total - 1)
    sent_stash = jnp.where(live_rows, stash[token_index], jnp.zeros((), stash.dtype))
    sent_stash = sent_stash.reshape(experts, capacity, feature_width)
    sent_scale = jnp.where(live_rows, scales[token_index], jnp.zeros((), scales.dtype))
    sent_scale = sent_scale.reshape(experts, capacity, blocks)
    weighted = gates.reshape(-1)[slot_index][:, None] * out_grad[token_index].astype(jnp.float32)
    sent_grad = jnp.where(live_rows, weighted, jnp.zeros((), jnp.float32)).astype(jnp.bfloat16)
    sent_grad = sent_grad.reshape(experts, capacity, feature_width)
    weight_in = w_gate_up[0]
    got_stash, got_scale, got_grad = (
        lax.all_to_all(sent_stash, "expert", split_axis=0, concat_axis=0, tiled=True),
        lax.all_to_all(sent_scale, "expert", split_axis=0, concat_axis=0, tiled=True),
        lax.all_to_all(sent_grad, "expert", split_axis=0, concat_axis=0, tiled=True),
    )
    features = dequantize(
        got_stash.reshape(row_total, feature_width), got_scale.reshape(row_total, blocks)
    )
    gate_up = jnp.dot(features, weight_in, preferred_element_type=jnp.float32)
    upstream = got_grad.reshape(row_total, feature_width)
    back_hidden = jnp.dot(
        upstream,
        lax.all_gather(w_down, "dp", axis=1, tiled=True)[0],
        preferred_element_type=jnp.float32,
    )
    hidden_grad = gated_backward(gate_up, back_hidden)
    slot_grads = lax.dot_general(
        hidden_grad, weight_in, (((1,), (1,)), ((), ())), preferred_element_type=jnp.float32
    ).astype(jnp.bfloat16)
    returned = lax.all_to_all(
        slot_grads.reshape(experts, capacity, feature_width),
        "expert",
        split_axis=0,
        concat_axis=0,
        tiled=True,
    )
    picked = returned.reshape(row_total, feature_width)[destination].astype(jnp.float32)
    input_grad = jnp.sum(picked.reshape(tokens, 2, feature_width), axis=1).astype(jnp.bfloat16)
    local_rows = feature_width // dp_count
    summed = lax.psum_scatter(
        lax.dot_general(
            features, hidden_grad, (((0,), (0,)), ((), ())), preferred_element_type=jnp.float32
        ).astype(jnp.bfloat16),
        "dp",
        scatter_dimension=0,
        tiled=True,
    ).astype(jnp.float32)
    grad_gate_up = (summed / dp_count).reshape(1, local_rows, 2 * hidden)
    return (input_grad, grad_gate_up)


def spec(shape, index):
    return pl.BlockSpec(shape, index)


def whole(array):
    rank = len(array.shape)
    return pl.BlockSpec(array.shape, lambda *_: (0,) * rank)


def cost(flops, *arrays):
    total = sum(math.prod(a.shape) * jnp.dtype(a.dtype).itemsize for a in arrays)
    return pl.CostEstimate(flops=flops, bytes_accessed=total, transcendentals=0)


def call(body, place, ins, outs, flops=0, grid=(1,), in_specs=None, out_specs=None, scratch=()):
    in_specs = in_specs or [whole(a) for a in ins]
    out_specs = out_specs or [whole(a) for a in outs]
    return pl.pallas_call(
        body,
        grid_spec=pltpu.PrefetchScalarGridSpec(
            num_scalar_prefetch=1,
            grid=grid,
            in_specs=in_specs,
            out_specs=out_specs,
            scratch_shapes=list(scratch),
        ),
        out_shape=outs,
        cost_estimate=cost(flops, *ins, *outs),
    )(place, *ins)


def shaped(shape, dtype):
    return jax.ShapeDtypeStruct(shape, dtype)


def prepare_grad(width, count, place, out_grad, gates, route_ids, sent, own_gate):
    other = 1 - place[1]
    for k in range(count):
        start = pl.multiple_of((2 * k + other) * width, 128)
        sent[:, k * width : (k + 1) * width] = out_grad[:, pl.ds(start, width)]
    first = route_ids[:, 0:1] == other
    theirs = jnp.where(first, gates[:, 0:1], gates[:, 1:2])
    mine = jnp.where(first, gates[:, 1:2], gates[:, 0:1])
    high = theirs.astype(jnp.bfloat16).astype(jnp.float32)
    rest = theirs - high
    lane = lax.broadcasted_iota(jnp.int32, own_gate.shape, 1)
    extra = jnp.where(lane == 0, high, jnp.where(lane == 1, rest, 0.0))
    sent[:, count * width :] = extra.astype(jnp.bfloat16)
    own_gate[...] = jnp.broadcast_to(mine, own_gate.shape)


def dequantize_body(block, place, stash, scales, features):
    for b in range(scales.shape[1]):
        cols = slice(b * block, (b + 1) * block)
        scaled = stash[:, cols].astype(jnp.float32) * scales[:, b : b + 1].astype(jnp.float32)
        features[:, cols] = scaled.astype(jnp.bfloat16)


def hidden_partial(width, relatives, place, out_grad, got_grad, *refs):
    pieces, total = refs[:-1], refs[-1]
    tokens = out_grad.shape[0]
    upper = jnp.zeros((tokens, total.shape[1]), jnp.float32)
    lower = upper
    for piece, pair in zip(pieces, relatives):
        for slot, relative in enumerate(pair):
            chip = (place[0] // 2) ^ relative
            here = pl.multiple_of((2 * chip + place[1]) * width, 128)
            there = pl.multiple_of(chip * width, 128)
            weight = piece[slot]
            upper += jnp.dot(out_grad[:, pl.ds(here, width)], weight, preferred_element_type=jnp.float32)
            lower += jnp.dot(got_grad[:, pl.ds(there, width)], weight, preferred_element_type=jnp.float32)
    total[:tokens] = upper
    total[tokens:] = lower


def hidden_select(width, relatives, place, out_grad, got_grad, ready, *refs):
    pieces, kept, sent, fresh = refs[:-3], refs[-3], refs[-2], refs[-1]
    hidden_partial(width, relatives, place, out_grad, got_grad, *pieces, fresh)
    tokens = out_grad.shape[0]
    swapped = lax.rem(place[0], 2) != place[1]
    kept[...] = jnp.where(swapped, fresh[...], ready[...])
    outgoing = jnp.where(swapped, ready[...], fresh[...]).astype(jnp.bfloat16)
    sent[:tokens] = outgoing[tokens:]
    sent[tokens:] = outgoing[:tokens]


def gated_body(place, own_up, got_up, kept, arrived, own_gate, got_grad, out):
    tokens, double = own_up.shape
    hidden = double // 2
    extra = got_grad[:, got_grad.shape[1] - 128 :].astype(jnp.float32)
    factors = (own_gate[:, 0:1], extra[:, 0:1] + extra[:, 1:2])
    for half, gate_up in enumerate((own_up, got_up)):
        rows = slice(half * tokens, (half + 1) * tokens)
        back = (kept[rows] + arrived[rows].astype(jnp.float32)) * factors[half]
        gate, up = gate_up[:, :hidden], gate_up[:, hidden:]
        sig = jax.nn.sigmoid(gate)
        out[rows, :hidden] = (back * up * sig * (1.0 + gate * (1.0 - sig))).astype(jnp.bfloat16)
        out[rows, hidden:] = (back * gate * sig).astype(jnp.bfloat16)


def weight_block(own, got, hidden_grad):
    tokens = own.shape[0]
    dims = (((0,), (0,)), ((), ()))
    total = lax.dot_general(own[...], hidden_grad[:tokens], dims, preferred_element_type=jnp.float32)
    return total + lax.dot_general(
        got[...], hidden_grad[tokens:], dims, preferred_element_type=jnp.float32
    )


def weight_first(place, own, got, hidden_grad, out):
    out[0] = weight_block(own, got, hidden_grad).astype(jnp.bfloat16)


def weight_add(scale, place, own, got, hidden_grad, *refs):
    out = refs[-1]
    total = weight_block(own, got, hidden_grad)
    for ref in refs[:-1]:
        part = ref[0] if len(ref.shape) == 3 else ref[...]
        total = total + part.astype(jnp.float32)
    out[...] = (total * scale).astype(out.dtype)


def dense_device(stash, scales, out_grad, route_ids, gates, w_gate_up, w_down):
    bf16, f32 = jnp.bfloat16, jnp.float32
    tokens, features_total = stash.shape
    blocks = scales.shape[1]
    width, hidden = w_down.shape[1:]
    double = 2 * hidden
    dp_count = lax.axis_size("dp")
    chips = dp_count // 2
    mine, plane = lax.axis_index("dp"), lax.axis_index("expert")
    place = jnp.stack([mine, plane]).astype(jnp.int32)
    weight_in = w_gate_up[0]

    def over_dp(value, bit):
        return lax.ppermute(value, "dp", [(i, i ^ bit) for i in range(dp_count)])

    def over_expert(value):
        return lax.ppermute(value, "expert", [(0, 1), (1, 0)])

    piece = lax.ppermute(
        w_down[0],
        ("dp", "expert"),
        [(2 * i + y, 2 * ((i & ~1) | y) + (i & 1)) for i in range(dp_count) for y in range(2)],
    )
    half = chips * width
    sent_grad, own_gate = call(
        functools.partial(prepare_grad, width, chips),
        place,
        (out_grad, gates, route_ids),
        (shaped((tokens, half + 128), bf16), shaped((tokens, 128), f32)),
    )
    got_grad = over_expert(sent_grad)
    (features,) = call(
        functools.partial(dequantize_body, features_total // blocks),
        place,
        (stash, scales),
        (shaped(stash.shape, bf16),),
    )
    got_features = over_expert(features)

    held = [piece] + [over_dp(piece, 4 * d) for d in range(1, dp_count // 4)]
    groups = [jnp.stack(held[s : s + 2]) for s in range(0, len(held), 2)]
    relatives = [(2 * s, 2 * s + 2) for s in range(0, len(held), 2)]
    groups = groups + [over_dp(g, 2) for g in groups]
    relatives = relatives + [tuple(r + 1 for r in pair) for pair in relatives]
    sibling = [over_dp(g, 1) for g in groups]
    flops = 4 * tokens * half * hidden
    (first_hidden,) = call(
        functools.partial(hidden_partial, width, relatives),
        place,
        (out_grad, got_grad, *groups),
        (shaped((2 * tokens, hidden), f32),),
        flops,
    )
    kept, sent_hidden = call(
        functools.partial(hidden_select, width, relatives),
        place,
        (out_grad, got_grad, first_hidden, *sibling),
        (shaped((2 * tokens, hidden), f32), shaped((2 * tokens, hidden), bf16)),
        flops,
        scratch=[pltpu.VMEM((2 * tokens, hidden), f32)],
    )
    got_hidden = over_expert(sent_hidden)
    own_up = jnp.dot(features, weight_in, preferred_element_type=f32)
    got_up = jnp.dot(got_features, weight_in, preferred_element_type=f32)
    (hidden_grad,) = call(
        gated_body,
        place,
        (own_up, got_up, kept, got_hidden, own_gate, got_grad),
        (shaped((2 * tokens, double), bf16),),
    )

    def slot_grad(rows):
        return lax.dot_general(
            rows, weight_in, (((1,), (1,)), ((), ())), preferred_element_type=f32
        ).astype(bf16)

    returned = over_expert(slot_grad(hidden_grad[tokens:]))

    def weight_call(body, relative, extra, extra_specs, outs, out_specs, steps):
        column = lambda s, place: (0, place[0] ^ relative(s))
        return call(
            body,
            place,
            (features, got_features, hidden_grad, *extra),
            outs,
            4 * tokens * width * double * steps,
            grid=(steps,),
            in_specs=[
                spec((tokens, width), column),
                spec((tokens, width), column),
                whole(hidden_grad),
                *extra_specs,
            ],
            out_specs=out_specs,
        )

    quarter = dp_count // 4
    slab = shaped((quarter, width, double), bf16)
    slab_block = lambda s: pl.BlockSpec((1, width, double), lambda _, place: (s, 0, 0))

    def first_slab(low):
        (slab_out,) = weight_call(
            weight_first,
            lambda s: 4 * (quarter - 1 - s) + low,
            (),
            [],
            (slab,),
            [spec((1, width, double), lambda s, place: (s, 0, 0))],
            quarter,
        )
        return over_dp(slab_out, 1)

    far, near = first_slab(3), first_slab(1)

    def added(relative, slab_in, extra, scale=1.0, dtype=bf16):
        (out,) = weight_call(
            functools.partial(weight_add, scale),
            lambda _: relative,
            (slab_in, *extra),
            [slab_block(quarter - 1 - relative // 4), *[whole(e) for e in extra]],
            (shaped((width, double), dtype),),
            [pl.BlockSpec((width, double), lambda _, place: (0, 0))],
            1,
        )
        return out

    across = {}
    for r in reversed(range(0, dp_count, 4)):
        across[r] = over_dp(added(r + 2, far, ()), 2)
    arrived = {r: [across[r]] for r in range(0, dp_count, 4)}
    order = sorted(range(4, dp_count, 4), key=lambda r: (r & -r, -r))
    for r in order:
        bit = r & -r
        arrived[r ^ bit].append(over_dp(added(r, near, arrived[r]), bit))
    grad = added(0, near, arrived[0], 1.0 / dp_count, f32)
    input_grad = (
        slot_grad(hidden_grad[:tokens]).astype(f32) + returned.astype(f32)
    ).astype(bf16)
    return input_grad, grad[None]


def solution(mesh):
    dp_count, experts = mesh.shape["dp"], mesh.shape["expert"]
    power = dp_count >= 8 and dp_count & (dp_count - 1) == 0

    def program(stash, scales, out_grad, route_ids, *rest):
        every = experts == route_ids.shape[1] == 2 and power
        body = dense_device if every else on_device
        return body(stash, scales, out_grad, route_ids, *rest)

    placed = (
        P(("dp", "expert"), None),
        P(("dp", "expert"), None),
        P(("dp", "expert"), None),
        P(("dp", "expert"), None),
        P(("dp", "expert"), None),
        P("expert", None, None),
        P("expert", "dp", None),
    )
    return jax.shard_map(
        program,
        mesh=mesh,
        in_specs=placed,
        out_specs=(P(("dp", "expert"), None), P("expert", "dp", None)),
        check_vma=False,
    )
```

```python
import functools
import math

import jax
import jax.numpy as jnp
from jax import lax
from jax.experimental import pallas as pl
from jax.experimental.pallas import tpu as pltpu
from jax.sharding import PartitionSpec as P


KERNEL_BYTES = 16 << 20


def dispatch_plan(route_ids, experts, capacity, tokens):
    flat_ids = route_ids.reshape(-1)
    onehot = (flat_ids[:, None] == jnp.arange(experts, dtype=jnp.int32)[None, :]).astype(jnp.int32)
    earlier = jnp.cumsum(onehot, axis=0) - onehot
    ranking = jnp.sum(earlier * onehot, axis=1)
    destination = flat_ids * capacity + ranking
    slot_total = 2 * tokens
    source = jnp.full((experts * capacity,), slot_total, jnp.int32)
    source = source.at[destination].set(jnp.arange(slot_total, dtype=jnp.int32))
    return (destination, source)


def dequantize(stash_rows, scale_rows):
    row_total = stash_rows.shape[0]
    blocks = scale_rows.shape[1]
    scaled = (
        stash_rows.reshape(row_total, blocks, -1).astype(jnp.float32)
        * scale_rows.astype(jnp.float32)[:, :, None]
    )
    return scaled.reshape(row_total, -1).astype(jnp.bfloat16)


def gated_backward(gate_up, back_hidden):
    hidden = back_hidden.shape[1]
    gate_value = gate_up[:, :hidden]
    up_value = gate_up[:, hidden:]
    sigmoid_gate = jax.nn.sigmoid(gate_value)
    grad_gate = back_hidden * up_value * sigmoid_gate * (1.0 + gate_value * (1.0 - sigmoid_gate))
    grad_up = back_hidden * gate_value * sigmoid_gate
    return jnp.concatenate([grad_gate, grad_up], axis=1).astype(jnp.bfloat16)


def on_device(stash, scales, out_grad, route_ids, gates, w_gate_up, w_down):
    tokens, feature_width = stash.shape
    blocks = scales.shape[1]
    hidden = w_down.shape[2]
    experts = lax.axis_size("expert")
    dp_count = lax.axis_size("dp")
    capacity = min(tokens, 7 * tokens // (2 * experts))
    row_total = experts * capacity
    destination, source = dispatch_plan(route_ids, experts, capacity, tokens)
    slot_total = 2 * tokens
    live_rows = (source < slot_total)[:, None]
    token_index = jnp.minimum(source // 2, tokens - 1)
    slot_index = jnp.minimum(source, slot_total - 1)
    sent_stash = jnp.where(live_rows, stash[token_index], jnp.zeros((), stash.dtype))
    sent_stash = sent_stash.reshape(experts, capacity, feature_width)
    sent_scale = jnp.where(live_rows, scales[token_index], jnp.zeros((), scales.dtype))
    sent_scale = sent_scale.reshape(experts, capacity, blocks)
    weighted = gates.reshape(-1)[slot_index][:, None] * out_grad[token_index].astype(jnp.float32)
    sent_grad = jnp.where(live_rows, weighted, jnp.zeros((), jnp.float32)).astype(jnp.bfloat16)
    sent_grad = sent_grad.reshape(experts, capacity, feature_width)
    weight_in = w_gate_up[0]
    got_stash, got_scale, got_grad = (
        lax.all_to_all(sent_stash, "expert", split_axis=0, concat_axis=0, tiled=True),
        lax.all_to_all(sent_scale, "expert", split_axis=0, concat_axis=0, tiled=True),
        lax.all_to_all(sent_grad, "expert", split_axis=0, concat_axis=0, tiled=True),
    )
    features = dequantize(
        got_stash.reshape(row_total, feature_width), got_scale.reshape(row_total, blocks)
    )
    gate_up = jnp.dot(features, weight_in, preferred_element_type=jnp.float32)
    upstream = got_grad.reshape(row_total, feature_width)
    back_hidden = jnp.dot(
        upstream,
        lax.all_gather(w_down, "dp", axis=1, tiled=True)[0],
        preferred_element_type=jnp.float32,
    )
    hidden_grad = gated_backward(gate_up, back_hidden)
    slot_grads = lax.dot_general(
        hidden_grad, weight_in, (((1,), (1,)), ((), ())), preferred_element_type=jnp.float32
    ).astype(jnp.bfloat16)
    returned = lax.all_to_all(
        slot_grads.reshape(experts, capacity, feature_width),
        "expert",
        split_axis=0,
        concat_axis=0,
        tiled=True,
    )
    picked = returned.reshape(row_total, feature_width)[destination].astype(jnp.float32)
    input_grad = jnp.sum(picked.reshape(tokens, 2, feature_width), axis=1).astype(jnp.bfloat16)
    local_rows = feature_width // dp_count
    summed = lax.psum_scatter(
        lax.dot_general(
            features, hidden_grad, (((0,), (0,)), ((), ())), preferred_element_type=jnp.float32
        ).astype(jnp.bfloat16),
        "dp",
        scatter_dimension=0,
        tiled=True,
    ).astype(jnp.float32)
    grad_gate_up = (summed / dp_count).reshape(1, local_rows, 2 * hidden)
    return (input_grad, grad_gate_up)


def call(body, ins, outs, flops=0):
    moved = sum(math.prod(a.shape) * jnp.dtype(a.dtype).itemsize for a in (*ins, *outs))
    kept = pl.BlockSpec(memory_space=pltpu.VMEM)
    return pl.pallas_call(
        body,
        in_specs=[kept for _ in ins],
        out_specs=[kept for _ in outs],
        out_shape=outs,
        cost_estimate=pl.CostEstimate(flops=flops, bytes_accessed=moved, transcendentals=0),
        compiler_params=pltpu.CompilerParams(vmem_limit_bytes=KERNEL_BYTES),
    )(*ins)


def shaped(shape, dtype):
    return jax.ShapeDtypeStruct(shape, dtype)


def prepare_grad(width, count, out_grad, gates, route_ids, sent, own_gate):
    other = 1 - lax.axis_index("expert")
    for k in range(count):
        start = pl.multiple_of((2 * k + other) * width, 128)
        sent[:, k * width : (k + 1) * width] = out_grad[:, pl.ds(start, width)]
    first = route_ids[0:1, :] == other
    theirs = jnp.where(first, gates[0:1, :], gates[1:2, :])
    mine = jnp.where(first, gates[1:2, :], gates[0:1, :])
    tokens = sent.shape[0]
    theirs, mine = (jnp.transpose(jnp.broadcast_to(row, (128, tokens))) for row in (theirs, mine))
    high = theirs.astype(jnp.bfloat16).astype(jnp.float32)
    lane = lax.broadcasted_iota(jnp.int32, own_gate.shape, 1)
    extra = jnp.where(lane == 0, high, jnp.where(lane == 1, theirs - high, 0.0))
    sent[:, count * width :] = extra.astype(jnp.bfloat16)
    own_gate[...] = mine


def dequantize_split(segment, stash, scales, near, far):
    side = lax.rem(lax.axis_index("dp") // 2, 2)
    block = stash.shape[1] // scales.shape[0]
    columns = jnp.transpose(scales[...].astype(jnp.float32))

    def fill(targets):
        for b in range(scales.shape[0]):
            chip, inside = divmod(b * block, segment)
            scaled = stash[:, b * block : (b + 1) * block].astype(jnp.float32)
            scaled = scaled * columns[:, b : b + 1]
            start = (chip // 2) * segment + inside
            targets[chip % 2][:, start : start + block] = scaled.astype(jnp.bfloat16)

    pl.when(side == 0)(lambda: fill((near, far)))
    pl.when(side == 1)(lambda: fill((far, near)))


def hidden_sums(width, relatives, out_grad, got_grad, pieces):
    mine, plane = lax.axis_index("dp") // 2, lax.axis_index("expert")
    upper = lower = None
    for piece, pair in zip(pieces, relatives):
        for slot, relative in enumerate(pair):
            chip = mine ^ relative
            here = pl.multiple_of((2 * chip + plane) * width, 128)
            there = pl.multiple_of(chip * width, 128)
            weight = piece[slot]
            one = jnp.dot(out_grad[:, pl.ds(here, width)], weight, preferred_element_type=jnp.float32)
            two = jnp.dot(got_grad[:, pl.ds(there, width)], weight, preferred_element_type=jnp.float32)
            upper = one if upper is None else upper + one
            lower = two if lower is None else lower + two
    return upper, lower


def hidden_first(width, relatives, out_grad, got_grad, *refs):
    tokens = out_grad.shape[0]
    upper, lower = hidden_sums(width, relatives, out_grad, got_grad, refs[:-1])
    refs[-1][:tokens] = upper
    refs[-1][tokens:] = lower


def hidden_select(width, relatives, out_grad, got_grad, ready, *refs):
    kept, sent = refs[-2:]
    tokens = out_grad.shape[0]
    upper, lower = hidden_sums(width, relatives, out_grad, got_grad, refs[:-2])
    swapped = lax.rem(lax.axis_index("dp"), 2) != lax.axis_index("expert")
    for fresh, here in ((upper, slice(0, tokens)), (lower, slice(tokens, 2 * tokens))):
        there = slice(tokens - here.start, 2 * tokens - here.start)
        old = ready[here]
        kept[here] = jnp.where(swapped, fresh, old)
        sent[there] = jnp.where(swapped, old, fresh).astype(jnp.bfloat16)


def feature_product(segment, features, weight_in, offset):
    side = lax.rem(lax.axis_index("dp") // 2 + offset, 2)
    total = None
    for chip in range(features.shape[1] // segment):
        rows = pl.multiple_of((2 * chip + side) * segment, 128)
        term = jnp.dot(
            features[:, chip * segment : (chip + 1) * segment],
            weight_in[pl.ds(rows, segment), :],
            preferred_element_type=jnp.float32,
        )
        total = term if total is None else total + term
    return total


def up_own(segment, near, far, weight_in, out):
    out[...] = feature_product(segment, near, weight_in, 0) + feature_product(segment, far, weight_in, 1)


def up_got(segment, far, weight_in, out):
    out[...] = feature_product(segment, far, weight_in, 1)


def gated_body(segment, near, weight_in, own_up, got_up, kept, arrived, own_gate, got_grad, out_gate, out_up):
    tokens, double = own_up.shape
    hidden = double // 2
    extra = got_grad[:, got_grad.shape[1] - 128 :].astype(jnp.float32)
    factors = (own_gate[:, 0:1], extra[:, 0:1] + extra[:, 1:2])
    others = got_up[...] + feature_product(segment, near, weight_in, 0)
    for half, gate_up in enumerate((own_up[...], others)):
        rows = slice(half * tokens, (half + 1) * tokens)
        back = (kept[rows] + arrived[rows].astype(jnp.float32)) * factors[half]
        gate, up = gate_up[:, :hidden], gate_up[:, hidden:]
        sig = jax.nn.sigmoid(gate)
        out_gate[rows] = (back * up * sig * (1.0 + gate * (1.0 - sig))).astype(jnp.bfloat16)
        out_up[rows] = (back * gate * sig).astype(jnp.bfloat16)


def combine_halves(*refs):
    parts, out = refs[:-1], refs[-1]
    count = len(parts) // 2
    for order in range(count):
        cols = slice(order * parts[order].shape[1], (order + 1) * parts[order].shape[1])
        total = parts[order][...].astype(jnp.float32) + parts[count + order][...].astype(jnp.float32)
        out[:, cols] = total.astype(out.dtype)


def slot_grads(first_row, first_col, grad_gate, grad_up, weight_in, out):
    tokens, total = out.shape
    hidden = grad_gate.shape[1]
    rows = slice(first_row, first_row + tokens)
    step = math.gcd(total, 512)
    for start in range(0, total, step):
        cols = slice(start, start + step)
        weight = weight_in[first_col + start : first_col + start + step]
        value = sum(
            lax.dot_general(g[rows], w, (((1,), (1,)), ((), ())), preferred_element_type=jnp.float32)
            for g, w in ((grad_gate, weight[:, :hidden]), (grad_up, weight[:, hidden:]))
        )
        out[:, cols] = value.astype(jnp.bfloat16)


def weight_block(count, width, relative, *refs):
    features, out = refs[:count], refs[-1]
    groups = out.shape[1] // refs[count].shape[1]
    grads, parts = refs[count : count + groups * (count // 2)], refs[count + groups * (count // 2) : -1]
    mine = lax.axis_index("dp")
    start = pl.multiple_of((2 * ((mine // 4) ^ relative) + lax.rem(mine, 2)) * width, 128)
    columns = jnp.concatenate([f[:, pl.ds(start, width)] for f in features], axis=0)
    wide = out.shape[1] // groups
    for group in range(groups):
        own = grads[group * (count // 2) : (group + 1) * (count // 2)]
        rows = jnp.concatenate([g[...] for g in own], axis=0)
        cols = slice(group * wide, (group + 1) * wide)
        total = lax.dot_general(
            columns, rows, (((0,), (0,)), ((), ())), preferred_element_type=jnp.float32
        )
        for part in parts:
            total = total + part[:, cols].astype(jnp.float32)
        out[:, cols] = total.astype(out.dtype)


def weight_last(scale, ready, *refs):
    parts, out = refs[:-1], refs[-1]
    wide = out.shape[1] // 2
    for group in range(2):
        cols = slice(group * wide, (group + 1) * wide)
        total = ready[:, cols]
        for part in parts[group::2]:
            total = total + part[...].astype(jnp.float32)
        out[:, cols] = total * scale


def dense_device(stash, scales, out_grad, route_ids, gates, w_gate_up, w_down):
    bf16, f32 = jnp.bfloat16, jnp.float32
    tokens, features_total = stash.shape
    width, hidden = w_down.shape[1:]
    double = 2 * hidden
    dp_count = lax.axis_size("dp")
    chips, deep = dp_count // 2, dp_count // 4
    segment, half = 2 * width, chips * width
    weight_in = w_gate_up[0]

    def over_dp(value, bit):
        return lax.ppermute(value, "dp", [(i, i ^ bit) for i in range(dp_count)])

    def over_expert(value):
        return lax.ppermute(value, "expert", [(0, 1), (1, 0)])

    def after(value, *others):
        return lax.optimization_barrier((value, *others))[0]

    piece = lax.ppermute(
        w_down[0],
        ("dp", "expert"),
        [(2 * i + y, 2 * ((i & ~1) | y) + (i & 1)) for i in range(dp_count) for y in range(2)],
    )
    near, far = call(
        functools.partial(dequantize_split, segment),
        (stash, scales.T),
        (shaped((tokens, half), bf16),) * 2,
    )
    got_far = over_expert(far)
    across_far = over_dp(far, 2)
    sent_grad, own_gate = call(
        functools.partial(prepare_grad, width, chips),
        (after(out_grad, far), gates.T, route_ids.T),
        (shaped((tokens, half + 128), bf16), shaped((tokens, 128), f32)),
    )
    got_grad = over_expert(sent_grad)
    got_near = over_expert(after(near, sent_grad))

    piece = after(piece, far)
    held = [piece] + [over_dp(piece, 4 * d) for d in range(1, deep)]
    groups = [jnp.stack(held[s : s + 2]) for s in range(0, deep, 2)]
    relatives = [(2 * s, 2 * s + 2) for s in range(0, deep, 2)]
    crossed = [over_dp(g, 2) for g in groups]
    groups = groups + crossed
    relatives = relatives + [tuple(r + 1 for r in pair) for pair in relatives]
    sibling = [over_dp(g, 1) for g in groups]
    across_got = over_dp(after(got_far, *crossed), 2)

    up_cost = tokens * features_total * double
    (own_up,) = call(
        functools.partial(up_own, segment),
        (near, far, weight_in),
        (shaped((tokens, double), f32),),
        2 * up_cost,
    )
    (got_up,) = call(
        functools.partial(up_got, segment),
        (got_far, weight_in),
        (shaped((tokens, double), f32),),
        up_cost,
    )
    flops = 4 * tokens * half * hidden
    (first_hidden,) = call(
        functools.partial(hidden_first, width, relatives),
        (out_grad, got_grad, *groups),
        (shaped((2 * tokens, hidden), f32),),
        flops,
    )
    kept, sent_hidden = call(
        functools.partial(hidden_select, width, relatives),
        (out_grad, got_grad, first_hidden, *sibling),
        (shaped((2 * tokens, hidden), f32), shaped((2 * tokens, hidden), bf16)),
        flops,
    )
    got_hidden = over_expert(sent_hidden)
    grad_gate, grad_up = call(
        functools.partial(gated_body, segment),
        (got_near, weight_in, own_up, got_up, kept, got_hidden, own_gate, got_grad),
        (shaped((2 * tokens, hidden), bf16),) * 2,
        up_cost,
    )
    grads = []
    for own in (grad_gate, grad_up):
        across = over_dp(own, 2)
        pair = [own, across]
        grads.append(pair + [over_dp(g, 1) for g in pair])
    shared = [near, got_near, across_far, across_got]
    shared = shared + [over_dp(f, 1) for f in shared]

    part_cols = features_total // 2
    returned = []
    for order in range(2):
        (sent_slots,) = call(
            functools.partial(slot_grads, tokens, order * part_cols),
            (grad_gate, grad_up, weight_in),
            (shaped((tokens, part_cols), bf16),),
            up_cost,
        )
        returned.append(over_expert(sent_slots))

    def block(relative, groups, parts, dtype=bf16):
        chosen = [g for group in groups for g in grads[group]]
        (out,) = call(
            functools.partial(weight_block, len(shared), width, relative),
            (*shared, *chosen, *parts),
            (shaped((width, hidden * len(groups)), dtype),),
            2 * len(shared) * tokens * width * hidden * len(groups),
        )
        return out

    top = deep // 2
    first_parts, last_parts = [], [[], []]
    arrived = {(r, g): [] for r in range(deep) for g in range(2)}
    for r in sorted(range(1, deep), key=lambda r: (r & -r, -r)):
        bit = r & -r
        if r == 1 != top:
            first_parts.append(over_dp(block(r, (0, 1), ()), 4 * bit))
            continue
        for g in range(2):
            moved = over_dp(block(r, (g,), arrived[r, g]), 4 * bit)
            (arrived[r ^ bit, g] if r != bit else last_parts[g]).append(moved)
    ready = block(0, (0, 1), first_parts, f32)
    (grad,) = call(
        functools.partial(weight_last, 1.0 / dp_count),
        (ready, *[p for pair in zip(*last_parts) for p in pair]),
        (shaped((width, double), f32),),
    )
    own_slots = []
    for order in range(2):
        (slots,) = call(
            functools.partial(slot_grads, 0, order * part_cols),
            (grad_gate, grad_up, weight_in),
            (shaped((tokens, part_cols), bf16),),
            up_cost,
        )
        own_slots.append(slots)
    (input_grad,) = call(combine_halves, (*own_slots, *returned), (shaped(stash.shape, bf16),))
    return input_grad, grad[None]


def solution(mesh):
    dp_count, experts = mesh.shape["dp"], mesh.shape["expert"]
    power = dp_count >= 8 and dp_count & (dp_count - 1) == 0

    def program(stash, scales, out_grad, route_ids, *rest):
        if not (experts == route_ids.shape[1] == 2 and power):
            return on_device(stash, scales, out_grad, route_ids, *rest)
        return dense_device(stash, scales, out_grad, route_ids, *rest)

    placed = (
        P(("dp", "expert"), None),
        P(("dp", "expert"), None),
        P(("dp", "expert"), None),
        P(("dp", "expert"), None),
        P(("dp", "expert"), None),
        P("expert", None, None),
        P("expert", "dp", None),
    )
    return jax.shard_map(
        program,
        mesh=mesh,
        in_specs=placed,
        out_specs=(P(("dp", "expert"), None), P("expert", "dp", None)),
        check_vma=False,
    )
```

```python
import functools
import math

import jax
import jax.numpy as jnp
from jax import lax
from jax.experimental import pallas as pl
from jax.experimental.pallas import tpu as pltpu
from jax.sharding import PartitionSpec as P


KERNEL_BYTES = 16 << 20


def dispatch_plan(route_ids, experts, capacity, tokens):
    flat_ids = route_ids.reshape(-1)
    onehot = (flat_ids[:, None] == jnp.arange(experts, dtype=jnp.int32)[None, :]).astype(jnp.int32)
    earlier = jnp.cumsum(onehot, axis=0) - onehot
    ranking = jnp.sum(earlier * onehot, axis=1)
    destination = flat_ids * capacity + ranking
    slot_total = 2 * tokens
    source = jnp.full((experts * capacity,), slot_total, jnp.int32)
    source = source.at[destination].set(jnp.arange(slot_total, dtype=jnp.int32))
    return (destination, source)


def dequantize(stash_rows, scale_rows):
    row_total = stash_rows.shape[0]
    blocks = scale_rows.shape[1]
    scaled = (
        stash_rows.reshape(row_total, blocks, -1).astype(jnp.float32)
        * scale_rows.astype(jnp.float32)[:, :, None]
    )
    return scaled.reshape(row_total, -1).astype(jnp.bfloat16)


def gated_backward(gate_up, back_hidden):
    hidden = back_hidden.shape[1]
    gate_value = gate_up[:, :hidden]
    up_value = gate_up[:, hidden:]
    sigmoid_gate = jax.nn.sigmoid(gate_value)
    grad_gate = back_hidden * up_value * sigmoid_gate * (1.0 + gate_value * (1.0 - sigmoid_gate))
    grad_up = back_hidden * gate_value * sigmoid_gate
    return jnp.concatenate([grad_gate, grad_up], axis=1).astype(jnp.bfloat16)


def on_device(stash, scales, out_grad, route_ids, gates, w_gate_up, w_down):
    tokens, feature_width = stash.shape
    blocks = scales.shape[1]
    hidden = w_down.shape[2]
    experts = lax.axis_size("expert")
    dp_count = lax.axis_size("dp")
    capacity = min(tokens, 7 * tokens // (2 * experts))
    row_total = experts * capacity
    destination, source = dispatch_plan(route_ids, experts, capacity, tokens)
    slot_total = 2 * tokens
    live_rows = (source < slot_total)[:, None]
    token_index = jnp.minimum(source // 2, tokens - 1)
    slot_index = jnp.minimum(source, slot_total - 1)
    sent_stash = jnp.where(live_rows, stash[token_index], jnp.zeros((), stash.dtype))
    sent_stash = sent_stash.reshape(experts, capacity, feature_width)
    sent_scale = jnp.where(live_rows, scales[token_index], jnp.zeros((), scales.dtype))
    sent_scale = sent_scale.reshape(experts, capacity, blocks)
    weighted = gates.reshape(-1)[slot_index][:, None] * out_grad[token_index].astype(jnp.float32)
    sent_grad = jnp.where(live_rows, weighted, jnp.zeros((), jnp.float32)).astype(jnp.bfloat16)
    sent_grad = sent_grad.reshape(experts, capacity, feature_width)
    weight_in = w_gate_up[0]
    got_stash, got_scale, got_grad = (
        lax.all_to_all(sent_stash, "expert", split_axis=0, concat_axis=0, tiled=True),
        lax.all_to_all(sent_scale, "expert", split_axis=0, concat_axis=0, tiled=True),
        lax.all_to_all(sent_grad, "expert", split_axis=0, concat_axis=0, tiled=True),
    )
    features = dequantize(
        got_stash.reshape(row_total, feature_width), got_scale.reshape(row_total, blocks)
    )
    gate_up = jnp.dot(features, weight_in, preferred_element_type=jnp.float32)
    upstream = got_grad.reshape(row_total, feature_width)
    back_hidden = jnp.dot(
        upstream,
        lax.all_gather(w_down, "dp", axis=1, tiled=True)[0],
        preferred_element_type=jnp.float32,
    )
    hidden_grad = gated_backward(gate_up, back_hidden)
    slot_grads = lax.dot_general(
        hidden_grad, weight_in, (((1,), (1,)), ((), ())), preferred_element_type=jnp.float32
    ).astype(jnp.bfloat16)
    returned = lax.all_to_all(
        slot_grads.reshape(experts, capacity, feature_width),
        "expert",
        split_axis=0,
        concat_axis=0,
        tiled=True,
    )
    picked = returned.reshape(row_total, feature_width)[destination].astype(jnp.float32)
    input_grad = jnp.sum(picked.reshape(tokens, 2, feature_width), axis=1).astype(jnp.bfloat16)
    local_rows = feature_width // dp_count
    summed = lax.psum_scatter(
        lax.dot_general(
            features, hidden_grad, (((0,), (0,)), ((), ())), preferred_element_type=jnp.float32
        ).astype(jnp.bfloat16),
        "dp",
        scatter_dimension=0,
        tiled=True,
    ).astype(jnp.float32)
    grad_gate_up = (summed / dp_count).reshape(1, local_rows, 2 * hidden)
    return (input_grad, grad_gate_up)


def call(body, ins, outs, flops=0):
    moved = sum(math.prod(a.shape) * jnp.dtype(a.dtype).itemsize for a in (*ins, *outs))
    kept = pl.BlockSpec(memory_space=pltpu.VMEM)
    return pl.pallas_call(
        body,
        in_specs=[kept for _ in ins],
        out_specs=[kept for _ in outs],
        out_shape=outs,
        cost_estimate=pl.CostEstimate(flops=flops, bytes_accessed=moved, transcendentals=0),
        compiler_params=pltpu.CompilerParams(vmem_limit_bytes=KERNEL_BYTES),
    )(*ins)


def shaped(shape, dtype):
    return jax.ShapeDtypeStruct(shape, dtype)


def prepare_grad(segment, out_grad, gates, route_ids, sent, own_gate, other_gate):
    other = 1 - lax.axis_index("expert")
    far_side = 1 - lax.rem(lax.axis_index("dp") // 2, 2)
    for k in range(sent.shape[1] // segment):
        start = pl.multiple_of((2 * k + far_side) * segment, 128)
        sent[:, k * segment : (k + 1) * segment] = out_grad[:, pl.ds(start, segment)]
    first = route_ids[0:1, :] == other
    theirs = jnp.where(first, gates[0:1, :], gates[1:2, :])
    mine = jnp.where(first, gates[1:2, :], gates[0:1, :])
    tokens = sent.shape[0]
    own_gate[...] = jnp.transpose(jnp.broadcast_to(mine, (128, tokens)))
    other_gate[...] = jnp.transpose(jnp.broadcast_to(theirs, (128, tokens)))


def z_half(deep):
    return lax.axis_index("dp") // (2 * deep)


def dequantize_split(segment, stash, scales, near, same, opposite):
    side = lax.rem(lax.axis_index("dp") // 2, 2)
    block = stash.shape[1] // scales.shape[0]
    deep = near.shape[1] // segment
    z_side = z_half(deep)
    columns = jnp.transpose(scales[...].astype(jnp.float32))

    def fill(x_here, z_here):
        for b in range(scales.shape[0]):
            chip, inside = divmod(b * block, segment)
            z, x = divmod(chip, 2)
            scaled = stash[:, b * block : (b + 1) * block].astype(jnp.float32)
            scaled = (scaled * columns[:, b : b + 1]).astype(jnp.bfloat16)
            half, within = divmod(z, deep // 2)
            target = near if x == x_here else same if half == z_here else opposite
            start = (z if x == x_here else within) * segment + inside
            target[:, start : start + block] = scaled

    for x_here in range(2):
        for z_here in range(2):
            pl.when((side == x_here) & (z_side == z_here))(functools.partial(fill, x_here, z_here))


def hidden_sums(width, relatives, out_grad, across, pieces):
    mine = lax.axis_index("dp")
    upper = lower = None
    for piece, relative in zip(pieces, relatives):
        block = mine ^ relative
        here = pl.multiple_of(block * width, 128)
        there = pl.multiple_of((2 * (block // 4) + lax.rem(block, 2)) * width, 128)
        weight = piece[...]
        one = jnp.dot(out_grad[:, pl.ds(here, width)], weight, preferred_element_type=jnp.float32)
        two = jnp.dot(across[:, pl.ds(there, width)], weight, preferred_element_type=jnp.float32)
        upper = one if upper is None else upper + one
        lower = two if lower is None else lower + two
    return upper, lower


def hidden_mine(width, relatives, out_grad, across, *refs):
    kept, passed = refs[-2:]
    kept[...], passed[...] = hidden_sums(width, relatives, out_grad, across, refs[:-2])


def hidden_other(width, relatives, out_grad, across, passed, *refs):
    kept, sent = refs[-2:]
    kept[...], lower = hidden_sums(width, relatives, out_grad, across, refs[:-2])
    hidden = kept.shape[1]
    sent[:, :hidden] = passed[...].astype(jnp.bfloat16)
    sent[:, hidden:] = lower.astype(jnp.bfloat16)


def hidden_finish(kept, arrived, gate, sent):
    hidden = kept.shape[1]
    total = kept[...] + arrived[:, hidden:].astype(jnp.float32)
    sent[...] = (total * gate[:, 0:1]).astype(jnp.bfloat16)


def feature_product(segment, features, weight_in, x_offset, z_offset):
    mine = lax.axis_index("dp")
    side = lax.rem(mine // 2 + x_offset, 2)
    count = features.shape[1] // segment
    base = 0 if z_offset is None else lax.rem(z_half(2 * count) + z_offset, 2) * count
    total = None
    for z in range(count):
        rows = pl.multiple_of((2 * (base + z) + side) * segment, 128)
        term = jnp.dot(
            features[:, z * segment : (z + 1) * segment],
            weight_in[pl.ds(rows, segment), :],
            preferred_element_type=jnp.float32,
        )
        total = term if total is None else total + term
    return total


def up_far(segment, same, opposite, weight_in, out):
    out[...] = feature_product(segment, same, weight_in, 1, 0) + feature_product(
        segment, opposite, weight_in, 1, 1
    )


def up_own(segment, near, same, opposite, weight_in, out):
    up_far(segment, same, opposite, weight_in, out)
    out[...] += feature_product(segment, near, weight_in, 0, None)


def gated_body(segment, near, weight_in, own_up, got_up, kept, across, arrived, own_gate, out_gate, out_up):
    tokens, double = own_up.shape
    hidden = double // 2
    own_back = (kept[...] + across[:, :hidden].astype(jnp.float32)) * own_gate[:, 0:1]
    got_back = arrived[...].astype(jnp.float32)
    others = got_up[...] + feature_product(segment, near, weight_in, 0, None)
    for half, (gate_up, back) in enumerate(((own_up[...], own_back), (others, got_back))):
        rows = slice(half * tokens, (half + 1) * tokens)
        gate, up = gate_up[:, :hidden], gate_up[:, hidden:]
        sig = jax.nn.sigmoid(gate)
        out_gate[rows] = (back * up * sig * (1.0 + gate * (1.0 - sig))).astype(jnp.bfloat16)
        out_up[rows] = (back * gate * sig).astype(jnp.bfloat16)


def combine_halves(*refs):
    parts, out = refs[:-1], refs[-1]
    count = len(parts) // 2
    for order in range(count):
        cols = slice(order * parts[order].shape[1], (order + 1) * parts[order].shape[1])
        total = parts[order][...].astype(jnp.float32) + parts[count + order][...].astype(jnp.float32)
        out[:, cols] = total.astype(out.dtype)


def slot_grads(first_row, first_col, grad_gate, grad_up, weight_in, out):
    tokens, total = out.shape
    hidden = grad_gate.shape[1]
    rows = slice(first_row, first_row + tokens)
    step = math.gcd(total, 512)
    for start in range(0, total, step):
        cols = slice(start, start + step)
        weight = weight_in[first_col + start : first_col + start + step]
        value = sum(
            lax.dot_general(g[rows], w, (((1,), (1,)), ((), ())), preferred_element_type=jnp.float32)
            for g, w in ((grad_gate, weight[:, :hidden]), (grad_up, weight[:, hidden:]))
        )
        out[:, cols] = value.astype(jnp.bfloat16)


def weight_block(count, width, relative, *refs):
    features, out = refs[:count], refs[-1]
    groups = out.shape[1] // refs[count].shape[1]
    grads, parts = refs[count : count + groups * (count // 2)], refs[count + groups * (count // 2) : -1]
    mine = lax.axis_index("dp")
    place = (2 * ((mine // 4) ^ relative) + lax.rem(mine, 2)) * width

    def block_of(array):
        start = pl.multiple_of(lax.rem(place, array.shape[1]), 128)
        return array[:, pl.ds(start, width)]

    columns = jnp.concatenate([block_of(f) for f in features], axis=0)
    wide = out.shape[1] // groups
    for group in range(groups):
        own = grads[group * (count // 2) : (group + 1) * (count // 2)]
        rows = jnp.concatenate([g[...] for g in own], axis=0)
        cols = slice(group * wide, (group + 1) * wide)
        total = lax.dot_general(
            columns, rows, (((0,), (0,)), ((), ())), preferred_element_type=jnp.float32
        )
        for part in parts:
            total = total + part[:, cols].astype(jnp.float32)
        out[:, cols] = total.astype(out.dtype)


def weight_last(scale, wholes, ready, *refs):
    parts, out = refs[:-1], refs[-1]
    wide = out.shape[1] // 2
    for group in range(2):
        cols = slice(group * wide, (group + 1) * wide)
        total = ready[:, cols]
        for part in parts[:wholes]:
            total = total + part[:, cols].astype(jnp.float32)
        for part in parts[wholes + group :: 2]:
            total = total + part[...].astype(jnp.float32)
        out[:, cols] = total * scale


def dense_device(stash, scales, out_grad, route_ids, gates, w_gate_up, w_down):
    bf16, f32 = jnp.bfloat16, jnp.float32
    tokens, features_total = stash.shape
    width, hidden = w_down.shape[1:]
    double = 2 * hidden
    dp_count = lax.axis_size("dp")
    deep = dp_count // 4
    segment, half = 2 * width, features_total // 2

    def over_dp(value, bit):
        return lax.ppermute(value, "dp", [(i, i ^ bit) for i in range(dp_count)])

    def over_expert(value):
        return lax.ppermute(value, "expert", [(0, 1), (1, 0)])

    def after(value, *others):
        return lax.optimization_barrier((value, *others))[0]

    piece = w_down[0]
    other_piece = over_expert(piece)
    distances = sorted(range(1, deep), reverse=True)
    pieces, relatives = [], [0] + [4 * d for d in distances]
    for own in (piece, other_piece):
        held = [own] + [over_dp(own, 4 * d) for d in distances]
        pieces.append(held + [over_dp(p, 1) for p in held])
    relatives = relatives + [r + 1 for r in relatives]

    sent_grad, own_gate, other_gate = call(
        functools.partial(prepare_grad, segment),
        (out_grad, gates.T, route_ids.T),
        (shaped((tokens, half), bf16), *(shaped((tokens, 128), f32),) * 2),
    )
    near, same, opposite = call(
        functools.partial(dequantize_split, segment),
        (after(stash, sent_grad), scales.T),
        (shaped((tokens, half), bf16), *(shaped((tokens, half // 2), bf16),) * 2),
    )
    weight_in = after(w_gate_up[0], near)
    got_opposite = over_expert(opposite)
    got_same = over_expert(same)
    got_near = over_expert(near)
    across_grad = over_dp(sent_grad, 2)
    across_opposite = over_dp(opposite, 2)
    across_got = over_dp(got_opposite, 2)

    up_cost = tokens * features_total * double
    (own_up,) = call(
        functools.partial(up_own, segment),
        (near, same, opposite, weight_in),
        (shaped((tokens, double), f32),),
        2 * up_cost,
    )
    (got_up,) = call(
        functools.partial(up_far, segment),
        (got_same, got_opposite, weight_in),
        (shaped((tokens, double), f32),),
        up_cost,
    )
    flops = 4 * tokens * half * hidden
    one = shaped((tokens, hidden), f32)
    kept_mine, passed = call(
        functools.partial(hidden_mine, width, relatives),
        (out_grad, across_grad, *pieces[0]),
        (one, one),
        flops,
    )
    kept_other, sent_sums = call(
        functools.partial(hidden_other, width, relatives),
        (out_grad, across_grad, passed, *pieces[1]),
        (one, shaped((tokens, double), bf16)),
        flops,
    )
    across_sums = over_dp(sent_sums, 2)
    (sent_hidden,) = call(
        hidden_finish, (kept_other, across_sums, other_gate), (shaped((tokens, hidden), bf16),)
    )
    got_hidden = over_expert(sent_hidden)
    grad_gate, grad_up = call(
        functools.partial(gated_body, segment),
        (got_near, weight_in, own_up, got_up, kept_mine, across_sums, got_hidden, own_gate),
        (shaped((2 * tokens, hidden), bf16),) * 2,
        up_cost,
    )

    grads = []
    for own in (grad_gate, grad_up):
        across = over_dp(own, 2)
        grads.append([own, across, over_dp(own, 1), over_dp(across, 1)])

    def with_core(arrays):
        return arrays + [over_dp(a, 1) for a in arrays]

    shared_near = with_core([near, got_near])
    shared_same = with_core([same, got_same])
    shared_far = with_core([across_opposite, across_got])
    quad = shared_near[:2] + shared_far[:2] + shared_near[2:] + shared_far[2:]

    part_cols = features_total // 2
    returned, own_slots = [], []
    for order in range(2):
        (sent_slots,) = call(
            functools.partial(slot_grads, tokens, order * part_cols),
            (grad_gate, grad_up, weight_in),
            (shaped((tokens, part_cols), bf16),),
            up_cost,
        )
        returned.append(over_expert(sent_slots))
        (slots,) = call(
            functools.partial(slot_grads, 0, order * part_cols),
            (grad_gate, grad_up, weight_in),
            (shaped((tokens, part_cols), bf16),),
            up_cost,
        )
        own_slots.append(slots)

    def block(relative, features, chosen, parts, dtype=bf16):
        wide = hidden * 2 * len(chosen) // len(features)
        (out,) = call(
            functools.partial(weight_block, len(features), width, relative),
            (*features, *chosen, *parts),
            (shaped((width, wide), dtype),),
            2 * len(features) * tokens * width * wide,
        )
        return out

    top = deep // 2
    dual = [g[n] for g in grads for n in (0, 2)]
    arrived = {r: [] for r in range(deep)}
    arrived_cols = {(r, g): [] for r in range(deep) for g in range(2)}
    for r in reversed(range(top)):
        arrived[r].append(over_dp(block(r, shared_same, dual, ()), 2))
    last_parts = [[], []]
    for r in sorted(range(1, deep), key=lambda r: (r & -r, -r)):
        bit = r & -r
        if r < top:
            arrived[r ^ bit].append(over_dp(block(r, shared_near, dual, arrived[r]), 4 * bit))
            continue
        for g in range(2):
            total = block(r, quad, grads[g], arrived_cols[r, g])
            moved = over_dp(total, 4 * bit)
            (arrived_cols[r ^ bit, g] if r != bit else last_parts[g]).append(moved)
    ready = block(0, shared_near, dual, arrived[0][:1], f32)
    wholes = arrived[0][1:]
    (grad,) = call(
        functools.partial(weight_last, 1.0 / dp_count, len(wholes)),
        (ready, *wholes, *[p for pair in zip(*last_parts) for p in pair]),
        (shaped((width, double), f32),),
    )
    (input_grad,) = call(combine_halves, (*own_slots, *returned), (shaped(stash.shape, bf16),))
    return input_grad, grad[None]


def solution(mesh):
    dp_count, experts = mesh.shape["dp"], mesh.shape["expert"]
    power = dp_count >= 8 and dp_count & (dp_count - 1) == 0

    def program(stash, scales, out_grad, route_ids, *rest):
        if not (experts == route_ids.shape[1] == 2 and power):
            return on_device(stash, scales, out_grad, route_ids, *rest)
        return dense_device(stash, scales, out_grad, route_ids, *rest)

    placed = (
        P(("dp", "expert"), None),
        P(("dp", "expert"), None),
        P(("dp", "expert"), None),
        P(("dp", "expert"), None),
        P(("dp", "expert"), None),
        P("expert", None, None),
        P("expert", "dp", None),
    )
    return jax.shard_map(
        program,
        mesh=mesh,
        in_specs=placed,
        out_specs=(P(("dp", "expert"), None), P("expert", "dp", None)),
        check_vma=False,
    )
```

```python
import functools
import math

import jax
import jax.numpy as jnp
from jax import lax
from jax.experimental import pallas as pl
from jax.experimental.pallas import tpu as pltpu
from jax.sharding import PartitionSpec as P


KERNEL_BYTES = 16 << 20


def dispatch_plan(route_ids, experts, capacity, tokens):
    flat_ids = route_ids.reshape(-1)
    onehot = (flat_ids[:, None] == jnp.arange(experts, dtype=jnp.int32)[None, :]).astype(jnp.int32)
    earlier = jnp.cumsum(onehot, axis=0) - onehot
    ranking = jnp.sum(earlier * onehot, axis=1)
    destination = flat_ids * capacity + ranking
    slot_total = 2 * tokens
    source = jnp.full((experts * capacity,), slot_total, jnp.int32)
    source = source.at[destination].set(jnp.arange(slot_total, dtype=jnp.int32))
    return (destination, source)


def dequantize(stash_rows, scale_rows):
    row_total = stash_rows.shape[0]
    blocks = scale_rows.shape[1]
    scaled = (
        stash_rows.reshape(row_total, blocks, -1).astype(jnp.float32)
        * scale_rows.astype(jnp.float32)[:, :, None]
    )
    return scaled.reshape(row_total, -1).astype(jnp.bfloat16)


def gated_backward(gate_up, back_hidden):
    hidden = back_hidden.shape[1]
    gate_value = gate_up[:, :hidden]
    up_value = gate_up[:, hidden:]
    sigmoid_gate = jax.nn.sigmoid(gate_value)
    grad_gate = back_hidden * up_value * sigmoid_gate * (1.0 + gate_value * (1.0 - sigmoid_gate))
    grad_up = back_hidden * gate_value * sigmoid_gate
    return jnp.concatenate([grad_gate, grad_up], axis=1).astype(jnp.bfloat16)


def on_device(stash, scales, out_grad, route_ids, gates, w_gate_up, w_down):
    tokens, feature_width = stash.shape
    blocks = scales.shape[1]
    hidden = w_down.shape[2]
    experts = lax.axis_size("expert")
    dp_count = lax.axis_size("dp")
    capacity = min(tokens, 7 * tokens // (2 * experts))
    row_total = experts * capacity
    destination, source = dispatch_plan(route_ids, experts, capacity, tokens)
    slot_total = 2 * tokens
    live_rows = (source < slot_total)[:, None]
    token_index = jnp.minimum(source // 2, tokens - 1)
    slot_index = jnp.minimum(source, slot_total - 1)
    sent_stash = jnp.where(live_rows, stash[token_index], jnp.zeros((), stash.dtype))
    sent_stash = sent_stash.reshape(experts, capacity, feature_width)
    sent_scale = jnp.where(live_rows, scales[token_index], jnp.zeros((), scales.dtype))
    sent_scale = sent_scale.reshape(experts, capacity, blocks)
    weighted = gates.reshape(-1)[slot_index][:, None] * out_grad[token_index].astype(jnp.float32)
    sent_grad = jnp.where(live_rows, weighted, jnp.zeros((), jnp.float32)).astype(jnp.bfloat16)
    sent_grad = sent_grad.reshape(experts, capacity, feature_width)
    weight_in = w_gate_up[0]
    got_stash, got_scale, got_grad = (
        lax.all_to_all(sent_stash, "expert", split_axis=0, concat_axis=0, tiled=True),
        lax.all_to_all(sent_scale, "expert", split_axis=0, concat_axis=0, tiled=True),
        lax.all_to_all(sent_grad, "expert", split_axis=0, concat_axis=0, tiled=True),
    )
    features = dequantize(
        got_stash.reshape(row_total, feature_width), got_scale.reshape(row_total, blocks)
    )
    gate_up = jnp.dot(features, weight_in, preferred_element_type=jnp.float32)
    upstream = got_grad.reshape(row_total, feature_width)
    back_hidden = jnp.dot(
        upstream,
        lax.all_gather(w_down, "dp", axis=1, tiled=True)[0],
        preferred_element_type=jnp.float32,
    )
    hidden_grad = gated_backward(gate_up, back_hidden)
    slot_grads = lax.dot_general(
        hidden_grad, weight_in, (((1,), (1,)), ((), ())), preferred_element_type=jnp.float32
    ).astype(jnp.bfloat16)
    returned = lax.all_to_all(
        slot_grads.reshape(experts, capacity, feature_width),
        "expert",
        split_axis=0,
        concat_axis=0,
        tiled=True,
    )
    picked = returned.reshape(row_total, feature_width)[destination].astype(jnp.float32)
    input_grad = jnp.sum(picked.reshape(tokens, 2, feature_width), axis=1).astype(jnp.bfloat16)
    local_rows = feature_width // dp_count
    summed = lax.psum_scatter(
        lax.dot_general(
            features, hidden_grad, (((0,), (0,)), ((), ())), preferred_element_type=jnp.float32
        ).astype(jnp.bfloat16),
        "dp",
        scatter_dimension=0,
        tiled=True,
    ).astype(jnp.float32)
    grad_gate_up = (summed / dp_count).reshape(1, local_rows, 2 * hidden)
    return (input_grad, grad_gate_up)


def call(body, ins, outs, flops=0):
    moved = sum(math.prod(a.shape) * jnp.dtype(a.dtype).itemsize for a in (*ins, *outs))
    kept = pl.BlockSpec(memory_space=pltpu.VMEM)
    return pl.pallas_call(
        body,
        in_specs=[kept for _ in ins],
        out_specs=[kept for _ in outs],
        out_shape=outs,
        cost_estimate=pl.CostEstimate(flops=flops, bytes_accessed=moved, transcendentals=0),
        compiler_params=pltpu.CompilerParams(vmem_limit_bytes=KERNEL_BYTES),
    )(*ins)


def fill_columns(body, ins, out, wide, filled):
    kept, away = pl.BlockSpec(memory_space=pltpu.VMEM), pl.BlockSpec(memory_space=pl.ANY)
    more = () if filled is None else (filled,)
    return pl.pallas_call(
        body,
        in_specs=[kept for _ in ins] + [away for _ in more],
        out_specs=away,
        out_shape=out,
        scratch_shapes=[pltpu.VMEM((out.shape[0], wide), out.dtype), pltpu.SemaphoreType.DMA],
        input_output_aliases={len(ins): 0} if more else {},
        compiler_params=pltpu.CompilerParams(vmem_limit_bytes=KERNEL_BYTES),
    )(*ins, *more)


def shaped(shape, dtype):
    return jax.ShapeDtypeStruct(shape, dtype)


def far_columns(segment, source, out, sem):
    far_side = 1 - lax.rem(lax.axis_index("dp") // 2, 2)
    copies = []
    for k in range(out.shape[1] // segment):
        start = pl.multiple_of((2 * k + far_side) * segment, 128)
        target = out.at[:, k * segment : (k + 1) * segment]
        copies.append(pltpu.make_async_copy(source.at[:, pl.ds(start, segment)], target, sem.at[k]))
        copies[k].start()
    for copy in copies:
        copy.wait()


def prepare_gates(gates, route_ids, own_gate, other_gate):
    first = route_ids[0:1, :] == lax.axis_index("expert")
    mine = jnp.where(first, gates[0:1, :], gates[1:2, :])
    theirs = jnp.where(first, gates[1:2, :], gates[0:1, :])
    own_gate[...] = jnp.transpose(jnp.broadcast_to(mine, (128, own_gate.shape[0])))
    other_gate[...] = jnp.broadcast_to(theirs, other_gate.shape)


def dequantize_split(segment, stash, scales, near, opposite, *same):
    mine = lax.axis_index("dp")
    block = stash.shape[1] // scales.shape[0]
    deep = near.shape[1] // segment
    columns = jnp.transpose(scales[...].astype(jnp.float32))

    def fill(x_here, z_here):
        for b in range(scales.shape[0]):
            chip, inside = divmod(b * block, segment)
            z, x = divmod(chip, 2)
            scaled = stash[:, b * block : (b + 1) * block].astype(jnp.float32)
            scaled = (scaled * columns[:, b : b + 1]).astype(jnp.bfloat16)
            if x == x_here:
                target, start = near, z * segment
            elif z ^ z_here < len(same):
                target, start = same[z ^ z_here], 0
            else:
                target, start = opposite, z % len(same) * segment
            target[:, start + inside : start + inside + block] = scaled

    for x_here in range(2):
        for z_here in range(deep):
            pl.when(mine // 2 == 2 * z_here + x_here)(functools.partial(fill, x_here, z_here))


def hidden_sums(width, relatives, out_grad, across, pieces):
    mine = lax.axis_index("dp")
    upper = lower = None
    for piece, relative in zip(pieces, relatives):
        block = mine ^ relative
        here = pl.multiple_of(block * width, 128)
        there = pl.multiple_of((2 * (block // 4) + lax.rem(block, 2)) * width, 128)
        weight = piece[...]
        one = jnp.dot(out_grad[:, pl.ds(here, width)], weight, preferred_element_type=jnp.float32)
        two = jnp.dot(across[:, pl.ds(there, width)], weight, preferred_element_type=jnp.float32)
        upper = one if upper is None else upper + one
        lower = two if lower is None else lower + two
    return upper, lower


def hidden_mine(width, relatives, out_grad, across, *refs):
    kept, passed = refs[-2:]
    kept[...], lower = hidden_sums(width, relatives, out_grad, across, refs[:-2])
    passed[...] = lower.astype(jnp.bfloat16)


def hidden_other(width, relatives, out_grad, across, *refs):
    direct, diagonal = refs[-2:]
    upper, lower = hidden_sums(width, relatives, out_grad, across, refs[:-2])
    direct[...] = upper.astype(jnp.bfloat16)
    diagonal[...] = lower.astype(jnp.bfloat16)


def feature_product(segment, features, weight_in, x_offset, base):
    side = lax.rem(lax.axis_index("dp") // 2 + x_offset, 2)
    total = None
    for k in range(features.shape[1] // segment):
        rows = pl.multiple_of((2 * (base + k) + side) * segment, 128)
        term = jnp.dot(
            features[:, k * segment : (k + 1) * segment],
            weight_in[pl.ds(rows, segment), :],
            preferred_element_type=jnp.float32,
        )
        total = term if total is None else total + term
    return total


def up_far(segment, weight_in, opposite, *refs):
    same, out = refs[:-1], refs[-1]
    z = lax.axis_index("dp") // 4
    total = feature_product(segment, opposite, weight_in, 1, len(same) - z // len(same) * len(same))
    for r, features in enumerate(same):
        total += feature_product(segment, features, weight_in, 1, z ^ r)
    out[...] = total


def up_own(segment, near, weight_in, *refs):
    up_far(segment, weight_in, *refs)
    refs[-1][...] += feature_product(segment, near, weight_in, 0, 0)


def gated_body(
    segment, near, weight_in, own_up, got_up, kept, across, direct, diagonal, own_gate, got_gate, out_gate, out_up
):
    tokens, double = own_up.shape
    hidden = double // 2
    own_back = (kept[...] + across[...].astype(jnp.float32)) * own_gate[:, 0:1]
    gates = jnp.transpose(jnp.broadcast_to(got_gate[0:1, :], (128, tokens)))
    got_back = (direct[...].astype(jnp.float32) + diagonal[...].astype(jnp.float32)) * gates[:, 0:1]
    others = got_up[...] + feature_product(segment, near, weight_in, 0, 0)
    for half, (gate_up, back) in enumerate(((own_up[...], own_back), (others, got_back))):
        rows = slice(half * tokens, (half + 1) * tokens)
        gate, up = gate_up[:, :hidden], gate_up[:, hidden:]
        sig = jax.nn.sigmoid(gate)
        out_gate[rows] = (back * up * sig * (1.0 + gate * (1.0 - sig))).astype(jnp.bfloat16)
        out_up[rows] = (back * gate * sig).astype(jnp.bfloat16)


def write_columns(start, out, rows, held, sem):
    held[...] = rows.astype(held.dtype)
    copy = pltpu.make_async_copy(held, out.at[:, pl.ds(start, held.shape[1])], sem)
    copy.start()
    copy.wait()


def combine_columns(start, own, got, *refs):
    write_columns(start, *refs[-3:-2], own[...].astype(jnp.float32) + got[...].astype(jnp.float32), *refs[-2:])


def weight_last(scale, wholes, ready, *refs):
    parts, out = refs[:-1], refs[-1]
    wide = out.shape[1] // 2
    for group in range(2):
        cols = slice(group * wide, (group + 1) * wide)
        total = ready[:, cols]
        for part in parts[:wholes]:
            total = total + part[:, cols].astype(jnp.float32)
        for part in parts[wholes + group :: 2]:
            total = total + part[...].astype(jnp.float32)
        out[:, cols] = total * scale


def slot_grads(first_row, first_col, grad_gate, grad_up, weight_in, out):
    tokens, total = out.shape
    hidden = grad_gate.shape[1]
    rows = slice(first_row, first_row + tokens)
    step = math.gcd(total, 512)
    for start in range(0, total, step):
        cols = slice(start, start + step)
        weight = weight_in[first_col + start : first_col + start + step]
        value = sum(
            lax.dot_general(g[rows], w, (((1,), (1,)), ((), ())), preferred_element_type=jnp.float32)
            for g, w in ((grad_gate, weight[:, :hidden]), (grad_up, weight[:, hidden:]))
        )
        out[:, cols] = value.astype(jnp.bfloat16)


def weight_block(count, width, relative, *refs):
    features, out = refs[:count], refs[-1]
    groups = out.shape[1] // refs[count].shape[1]
    grads, parts = refs[count : count + groups * (count // 2)], refs[count + groups * (count // 2) : -1]
    mine = lax.axis_index("dp")
    place = (2 * ((mine // 4) ^ relative) + lax.rem(mine, 2)) * width

    def block_of(array):
        start = pl.multiple_of(lax.rem(place, array.shape[1]), 128)
        return array[:, pl.ds(start, width)]

    columns = jnp.concatenate([block_of(f) for f in features], axis=0)
    wide = out.shape[1] // groups
    for group in range(groups):
        own = grads[group * (count // 2) : (group + 1) * (count // 2)]
        rows = jnp.concatenate([g[...] for g in own], axis=0)
        cols = slice(group * wide, (group + 1) * wide)
        total = lax.dot_general(
            columns, rows, (((0,), (0,)), ((), ())), preferred_element_type=jnp.float32
        )
        for part in parts:
            total = total + part[:, cols].astype(jnp.float32)
        out[:, cols] = total.astype(out.dtype)


def dense_device(stash, scales, out_grad, route_ids, gates, w_gate_up, w_down):
    bf16, f32 = jnp.bfloat16, jnp.float32
    tokens, features_total = stash.shape
    width, hidden = w_down.shape[1:]
    double = 2 * hidden
    dp_count = lax.axis_size("dp")
    deep = dp_count // 4
    segment, half = 2 * width, features_total // 2

    def over_dp(value, bit):
        return lax.ppermute(value, "dp", [(i, i ^ bit) for i in range(dp_count)])

    def over_expert(value):
        return lax.ppermute(value, "expert", [(0, 1), (1, 0)])

    def after(value, *others):
        return lax.optimization_barrier((value, *others))[0]

    piece = w_down[0]
    other_piece = over_expert(piece)
    bits = [1 << b for b in reversed(range(deep.bit_length() - 1))]
    pieces = []
    for own in (piece, other_piece):
        held = {0: own}
        for bit in bits:
            held.update({r | bit: over_dp(p, 4 * bit) for r, p in held.items()})
        relatives = [4 * r for r in held]
        held = list(held.values())
        pieces.append(held + [over_dp(p, 1) for p in held])
    relatives = relatives + [r + 1 for r in relatives]

    sent_grad = pl.pallas_call(
        functools.partial(far_columns, segment),
        in_specs=[pl.BlockSpec(memory_space=pltpu.HBM)],
        out_specs=pl.BlockSpec(memory_space=pltpu.VMEM),
        out_shape=shaped((tokens, half), bf16),
        scratch_shapes=[pltpu.SemaphoreType.DMA((deep,))],
        compiler_params=pltpu.CompilerParams(vmem_limit_bytes=KERNEL_BYTES),
    )(out_grad)
    own_gate, other_gate = call(
        prepare_gates,
        (gates.T, after(route_ids.T, sent_grad)),
        (shaped((tokens, 128), f32), shaped((8, tokens), f32)),
    )
    got_gate = over_expert(other_gate)
    near, opposite, *same = call(
        functools.partial(dequantize_split, segment),
        (after(stash, sent_grad), scales.T),
        (
            shaped((tokens, half), bf16),
            shaped((tokens, half // 2), bf16),
            *(shaped((tokens, segment), bf16),) * (deep // 2),
        ),
    )
    weight_in = after(w_gate_up[0], near)
    got_opposite = over_expert(opposite)
    got_same = [over_expert(f) for f in same]
    got_near = over_expert(near)
    across_grad = over_dp(sent_grad, 2)
    across_opposite = over_dp(opposite, 2)
    across_got = over_dp(got_opposite, 2)
    across_same = [over_dp(f, 2) for f in same[1:]]
    across_got_same = [over_dp(f, 2) for f in got_same[1:]]

    up_cost = tokens * features_total * double
    (own_up,) = call(
        functools.partial(up_own, segment),
        (near, weight_in, opposite, *same),
        (shaped((tokens, double), f32),),
        2 * up_cost,
    )
    (got_up,) = call(
        functools.partial(up_far, segment),
        (weight_in, got_opposite, *got_same),
        (shaped((tokens, double), f32),),
        up_cost,
    )
    flops = 4 * tokens * half * hidden
    sums = shaped((tokens, hidden), bf16)
    kept, passed = call(
        functools.partial(hidden_mine, width, relatives),
        (out_grad, across_grad, *pieces[0]),
        (shaped((tokens, hidden), f32), sums),
        flops,
    )
    across_hidden = over_dp(passed, 2)
    direct, diagonal = call(
        functools.partial(hidden_other, width, relatives),
        (out_grad, across_grad, *pieces[1]),
        (sums, sums),
        flops,
    )
    got_direct = over_expert(direct)
    got_diagonal = lax.ppermute(
        diagonal,
        ("dp", "expert"),
        [(2 * i + y, 2 * (i ^ 2) + 1 - y) for i in range(dp_count) for y in range(2)],
    )
    grad_gate, grad_up = call(
        functools.partial(gated_body, segment),
        (got_near, weight_in, own_up, got_up, kept, across_hidden, got_direct, got_diagonal, own_gate, got_gate),
        (shaped((2 * tokens, hidden), bf16),) * 2,
        up_cost,
    )

    grads = []
    for own in (grad_gate, grad_up):
        across = over_dp(own, 2)
        grads.append([own, across, over_dp(own, 1), over_dp(across, 1)])

    def with_core(arrays):
        return arrays + [over_dp(a, 1) for a in arrays]

    shared_near = with_core([near, got_near])
    shared_self = with_core([same[0], got_same[0]])
    shared_far = with_core([across_opposite, across_got])
    shared_same = [with_core(list(pair)) for pair in zip(across_same, across_got_same)]

    returned, own_slots = [], []
    quarter = half // 2
    parts = ((0, quarter), (quarter, half), (half + quarter, quarter))
    for first_col, part_cols in parts:
        (sent_slots,) = call(
            functools.partial(slot_grads, tokens, first_col),
            (grad_gate, grad_up, weight_in),
            (shaped((tokens, part_cols), bf16),),
            up_cost,
        )
        returned.append(over_expert(sent_slots))
        (slots,) = call(
            functools.partial(slot_grads, 0, first_col),
            (grad_gate, grad_up, weight_in),
            (shaped((tokens, part_cols), bf16),),
            up_cost,
        )
        own_slots.append(slots)

    def block(relative, features, chosen, parts, dtype=bf16):
        wide = hidden * 2 * len(chosen) // len(features)
        (out,) = call(
            functools.partial(weight_block, len(features), width, relative),
            (*features, *chosen, *parts),
            (shaped((width, wide), dtype),),
            2 * len(features) * tokens * width * wide,
        )
        return out

    top = deep // 2
    dual = [g[n] for g in grads for n in (0, 2)]
    across = over_dp(block(0, shared_self, dual, ()), 2)
    wholes, last_parts = [], [[], []]
    arrived = {(r, g): [] for r in range(deep) for g in range(2)}
    for r in sorted(range(1, deep), key=lambda r: (r & -r, -r)):
        bit = r & -r
        far = shared_far if r >= top else shared_same[r - 1]
        quad = shared_near[:2] + far[:2] + shared_near[2:] + far[2:]
        if r == 1:
            wholes.append(over_dp(block(r, quad, grads[0] + grads[1], ()), 4 * bit))
            continue
        for g in range(2):
            total = block(r, quad, grads[g], arrived[r, g])
            moved = over_dp(total, 4 * bit)
            (arrived[r ^ bit, g] if r != bit else last_parts[g]).append(moved)
    ready = block(0, shared_near, dual, (across,), f32)
    (grad,) = call(
        functools.partial(weight_last, 1.0 / dp_count, len(wholes)),
        (ready, *wholes, *[p for pair in zip(*last_parts) for p in pair]),
        (shaped((width, double), f32),),
    )
    input_grad = None
    for order, (first_col, part_cols) in enumerate(parts):
        input_grad = fill_columns(
            functools.partial(combine_columns, first_col),
            (own_slots[order], returned[order]),
            shaped(stash.shape, bf16),
            part_cols,
            input_grad,
        )
    return input_grad, grad[None]


def solution(mesh):
    dp_count, experts = mesh.shape["dp"], mesh.shape["expert"]
    power = dp_count >= 16 and dp_count & (dp_count - 1) == 0

    def program(stash, scales, out_grad, route_ids, *rest):
        if not (experts == route_ids.shape[1] == 2 and power):
            return on_device(stash, scales, out_grad, route_ids, *rest)
        return dense_device(stash, scales, out_grad, route_ids, *rest)

    placed = (
        P(("dp", "expert"), None),
        P(("dp", "expert"), None),
        P(("dp", "expert"), None),
        P(("dp", "expert"), None),
        P(("dp", "expert"), None),
        P("expert", None, None),
        P("expert", "dp", None),
    )
    return jax.shard_map(
        program,
        mesh=mesh,
        in_specs=placed,
        out_specs=(P(("dp", "expert"), None), P("expert", "dp", None)),
        check_vma=False,
    )
```

```python
import functools
import math

import jax
import jax.numpy as jnp
from jax import lax
from jax.experimental import pallas as pl
from jax.experimental.pallas import tpu as pltpu
from jax.sharding import PartitionSpec as P


KERNEL_BYTES = 16 << 20


def dispatch_plan(route_ids, experts, capacity, tokens):
    flat_ids = route_ids.reshape(-1)
    onehot = (flat_ids[:, None] == jnp.arange(experts, dtype=jnp.int32)[None, :]).astype(jnp.int32)
    earlier = jnp.cumsum(onehot, axis=0) - onehot
    ranking = jnp.sum(earlier * onehot, axis=1)
    destination = flat_ids * capacity + ranking
    slot_total = 2 * tokens
    source = jnp.full((experts * capacity,), slot_total, jnp.int32)
    source = source.at[destination].set(jnp.arange(slot_total, dtype=jnp.int32))
    return (destination, source)


def dequantize(stash_rows, scale_rows):
    row_total = stash_rows.shape[0]
    blocks = scale_rows.shape[1]
    scaled = (
        stash_rows.reshape(row_total, blocks, -1).astype(jnp.float32)
        * scale_rows.astype(jnp.float32)[:, :, None]
    )
    return scaled.reshape(row_total, -1).astype(jnp.bfloat16)


def gated_backward(gate_up, back_hidden):
    hidden = back_hidden.shape[1]
    gate_value = gate_up[:, :hidden]
    up_value = gate_up[:, hidden:]
    sigmoid_gate = jax.nn.sigmoid(gate_value)
    grad_gate = back_hidden * up_value * sigmoid_gate * (1.0 + gate_value * (1.0 - sigmoid_gate))
    grad_up = back_hidden * gate_value * sigmoid_gate
    return jnp.concatenate([grad_gate, grad_up], axis=1).astype(jnp.bfloat16)


def on_device(stash, scales, out_grad, route_ids, gates, w_gate_up, w_down):
    tokens, feature_width = stash.shape
    blocks = scales.shape[1]
    hidden = w_down.shape[2]
    experts = lax.axis_size("expert")
    dp_count = lax.axis_size("dp")
    capacity = min(tokens, 7 * tokens // (2 * experts))
    row_total = experts * capacity
    destination, source = dispatch_plan(route_ids, experts, capacity, tokens)
    slot_total = 2 * tokens
    live_rows = (source < slot_total)[:, None]
    token_index = jnp.minimum(source // 2, tokens - 1)
    slot_index = jnp.minimum(source, slot_total - 1)
    sent_stash = jnp.where(live_rows, stash[token_index], jnp.zeros((), stash.dtype))
    sent_stash = sent_stash.reshape(experts, capacity, feature_width)
    sent_scale = jnp.where(live_rows, scales[token_index], jnp.zeros((), scales.dtype))
    sent_scale = sent_scale.reshape(experts, capacity, blocks)
    weighted = gates.reshape(-1)[slot_index][:, None] * out_grad[token_index].astype(jnp.float32)
    sent_grad = jnp.where(live_rows, weighted, jnp.zeros((), jnp.float32)).astype(jnp.bfloat16)
    sent_grad = sent_grad.reshape(experts, capacity, feature_width)
    weight_in = w_gate_up[0]
    got_stash, got_scale, got_grad = (
        lax.all_to_all(sent_stash, "expert", split_axis=0, concat_axis=0, tiled=True),
        lax.all_to_all(sent_scale, "expert", split_axis=0, concat_axis=0, tiled=True),
        lax.all_to_all(sent_grad, "expert", split_axis=0, concat_axis=0, tiled=True),
    )
    features = dequantize(
        got_stash.reshape(row_total, feature_width), got_scale.reshape(row_total, blocks)
    )
    gate_up = jnp.dot(features, weight_in, preferred_element_type=jnp.float32)
    upstream = got_grad.reshape(row_total, feature_width)
    back_hidden = jnp.dot(
        upstream,
        lax.all_gather(w_down, "dp", axis=1, tiled=True)[0],
        preferred_element_type=jnp.float32,
    )
    hidden_grad = gated_backward(gate_up, back_hidden)
    slot_grads = lax.dot_general(
        hidden_grad, weight_in, (((1,), (1,)), ((), ())), preferred_element_type=jnp.float32
    ).astype(jnp.bfloat16)
    returned = lax.all_to_all(
        slot_grads.reshape(experts, capacity, feature_width),
        "expert",
        split_axis=0,
        concat_axis=0,
        tiled=True,
    )
    picked = returned.reshape(row_total, feature_width)[destination].astype(jnp.float32)
    input_grad = jnp.sum(picked.reshape(tokens, 2, feature_width), axis=1).astype(jnp.bfloat16)
    local_rows = feature_width // dp_count
    summed = lax.psum_scatter(
        lax.dot_general(
            features, hidden_grad, (((0,), (0,)), ((), ())), preferred_element_type=jnp.float32
        ).astype(jnp.bfloat16),
        "dp",
        scatter_dimension=0,
        tiled=True,
    ).astype(jnp.float32)
    grad_gate_up = (summed / dp_count).reshape(1, local_rows, 2 * hidden)
    return (input_grad, grad_gate_up)


def call(body, ins, outs, flops=0):
    moved = sum(math.prod(a.shape) * jnp.dtype(a.dtype).itemsize for a in (*ins, *outs))
    kept = pl.BlockSpec(memory_space=pltpu.VMEM)
    return pl.pallas_call(
        body,
        in_specs=[kept for _ in ins],
        out_specs=[kept for _ in outs],
        out_shape=outs,
        cost_estimate=pl.CostEstimate(flops=flops, bytes_accessed=moved, transcendentals=0),
        compiler_params=pltpu.CompilerParams(vmem_limit_bytes=KERNEL_BYTES),
    )(*ins)


def fill_columns(body, ins, out, wide, filled):
    kept, away = pl.BlockSpec(memory_space=pltpu.VMEM), pl.BlockSpec(memory_space=pl.ANY)
    more = () if filled is None else (filled,)
    return pl.pallas_call(
        body,
        in_specs=[kept for _ in ins] + [away for _ in more],
        out_specs=away,
        out_shape=out,
        scratch_shapes=[pltpu.VMEM((out.shape[0], wide), out.dtype), pltpu.SemaphoreType.DMA],
        input_output_aliases={len(ins): 0} if more else {},
        compiler_params=pltpu.CompilerParams(vmem_limit_bytes=KERNEL_BYTES),
    )(*ins, *more)


def shaped(shape, dtype):
    return jax.ShapeDtypeStruct(shape, dtype)


def far_columns(segment, source, out, sem):
    far_side = 1 - lax.rem(lax.axis_index("dp") // 2, 2)
    copies = []
    for k in range(out.shape[1] // segment):
        start = pl.multiple_of((2 * k + far_side) * segment, 128)
        target = out.at[:, k * segment : (k + 1) * segment]
        copies.append(pltpu.make_async_copy(source.at[:, pl.ds(start, segment)], target, sem.at[k]))
        copies[k].start()
    for copy in copies:
        copy.wait()


def prepare_gates(gates, route_ids, own_gate, other_gate):
    first = route_ids[0:1, :] == lax.axis_index("expert")
    mine = jnp.where(first, gates[0:1, :], gates[1:2, :])
    theirs = jnp.where(first, gates[1:2, :], gates[0:1, :])
    own_gate[...] = jnp.transpose(jnp.broadcast_to(mine, (128, own_gate.shape[0])))
    other_gate[...] = jnp.broadcast_to(theirs, other_gate.shape)


def dequantize_split(segment, stash, scales, near, opposite, *same):
    mine = lax.axis_index("dp")
    block = stash.shape[1] // scales.shape[0]
    deep = near.shape[1] // segment
    columns = jnp.transpose(scales[...].astype(jnp.float32))

    def fill(x_here, z_here):
        for b in range(scales.shape[0]):
            chip, inside = divmod(b * block, segment)
            z, x = divmod(chip, 2)
            scaled = stash[:, b * block : (b + 1) * block].astype(jnp.float32)
            scaled = (scaled * columns[:, b : b + 1]).astype(jnp.bfloat16)
            if x == x_here:
                target, start = near, z * segment
            elif z ^ z_here < len(same):
                target, start = same[z ^ z_here], 0
            else:
                target, start = opposite, z % len(same) * segment
            target[:, start + inside : start + inside + block] = scaled

    for x_here in range(2):
        for z_here in range(deep):
            pl.when(mine // 2 == 2 * z_here + x_here)(functools.partial(fill, x_here, z_here))


def hidden_sums(width, relatives, out_grad, across, pieces):
    mine = lax.axis_index("dp")
    upper = lower = None
    for piece, relative in zip(pieces, relatives):
        block = mine ^ relative
        here = pl.multiple_of(block * width, 128)
        there = pl.multiple_of((2 * (block // 4) + lax.rem(block, 2)) * width, 128)
        weight = piece[...]
        one = jnp.dot(out_grad[:, pl.ds(here, width)], weight, preferred_element_type=jnp.float32)
        two = jnp.dot(across[:, pl.ds(there, width)], weight, preferred_element_type=jnp.float32)
        upper = one if upper is None else upper + one
        lower = two if lower is None else lower + two
    return upper, lower


def hidden_mine(width, relatives, out_grad, across, *refs):
    kept, passed = refs[-2:]
    kept[...], lower = hidden_sums(width, relatives, out_grad, across, refs[:-2])
    passed[...] = lower.astype(jnp.bfloat16)


def hidden_other(width, relatives, out_grad, across, *refs):
    direct, diagonal = refs[-2:]
    upper, lower = hidden_sums(width, relatives, out_grad, across, refs[:-2])
    direct[...] = upper.astype(jnp.bfloat16)
    diagonal[...] = lower.astype(jnp.bfloat16)


def feature_product(segment, features, weight_in, x_offset, base):
    side = lax.rem(lax.axis_index("dp") // 2 + x_offset, 2)
    total = None
    for k in range(features.shape[1] // segment):
        rows = pl.multiple_of((2 * (base + k) + side) * segment, 128)
        term = jnp.dot(
            features[:, k * segment : (k + 1) * segment],
            weight_in[pl.ds(rows, segment), :],
            preferred_element_type=jnp.float32,
        )
        total = term if total is None else total + term
    return total


def up_far(segment, weight_in, opposite, *refs):
    same, out = refs[:-1], refs[-1]
    z = lax.axis_index("dp") // 4
    total = feature_product(segment, opposite, weight_in, 1, len(same) - z // len(same) * len(same))
    for r, features in enumerate(same):
        total += feature_product(segment, features, weight_in, 1, z ^ r)
    out[...] = total


def up_own(segment, near, weight_in, *refs):
    up_far(segment, weight_in, *refs)
    refs[-1][...] += feature_product(segment, near, weight_in, 0, 0)


def gated_body(
    segment, near, weight_in, own_up, got_up, kept, across, direct, diagonal, own_gate, got_gate, out_gate, out_up
):
    tokens, double = own_up.shape
    hidden = double // 2
    own_back = (kept[...] + across[...].astype(jnp.float32)) * own_gate[:, 0:1]
    gates = jnp.transpose(jnp.broadcast_to(got_gate[0:1, :], (128, tokens)))
    got_back = (direct[...].astype(jnp.float32) + diagonal[...].astype(jnp.float32)) * gates[:, 0:1]
    others = got_up[...] + feature_product(segment, near, weight_in, 0, 0)
    for half, (gate_up, back) in enumerate(((own_up[...], own_back), (others, got_back))):
        rows = slice(half * tokens, (half + 1) * tokens)
        gate, up = gate_up[:, :hidden], gate_up[:, hidden:]
        sig = jax.nn.sigmoid(gate)
        out_gate[rows] = (back * up * sig * (1.0 + gate * (1.0 - sig))).astype(jnp.bfloat16)
        out_up[rows] = (back * gate * sig).astype(jnp.bfloat16)


def write_columns(start, out, rows, held, sem):
    held[...] = rows.astype(held.dtype)
    copy = pltpu.make_async_copy(held, out.at[:, pl.ds(start, held.shape[1])], sem)
    copy.start()
    copy.wait()


def combine_columns(start, own, got, *refs):
    write_columns(start, *refs[-3:-2], own[...].astype(jnp.float32) + got[...].astype(jnp.float32), *refs[-2:])


def weight_last(scale, wholes, ready, *refs):
    parts, out, held, sem = refs[:-3], *refs[-3:]
    wide = out.shape[1] // 2
    copies = []
    for group in range(2):
        cols = slice(group * wide, (group + 1) * wide)
        total = ready[:, cols]
        for part in parts[:wholes]:
            total = total + part[:, cols].astype(jnp.float32)
        for part in parts[wholes + group :: 2]:
            total = total + part[...].astype(jnp.float32)
        held[group] = total * scale
        copies.append(pltpu.make_async_copy(held.at[group], out.at[:, cols], sem.at[group]))
        copies[group].start()
    for copy in copies:
        copy.wait()


def slot_grads(first_row, first_col, grad_gate, grad_up, weight_in, out):
    tokens, total = out.shape
    hidden = grad_gate.shape[1]
    rows = slice(first_row, first_row + tokens)
    step = math.gcd(total, 512)
    for start in range(0, total, step):
        cols = slice(start, start + step)
        weight = weight_in[first_col + start : first_col + start + step]
        value = sum(
            lax.dot_general(g[rows], w, (((1,), (1,)), ((), ())), preferred_element_type=jnp.float32)
            for g, w in ((grad_gate, weight[:, :hidden]), (grad_up, weight[:, hidden:]))
        )
        out[:, cols] = value.astype(jnp.bfloat16)


def weight_block(count, width, relative, *refs):
    features, out = refs[:count], refs[-1]
    groups = out.shape[1] // refs[count].shape[1]
    grads, parts = refs[count : count + groups * (count // 2)], refs[count + groups * (count // 2) : -1]
    mine = lax.axis_index("dp")
    place = (2 * ((mine // 4) ^ relative) + lax.rem(mine, 2)) * width

    def block_of(array):
        start = pl.multiple_of(lax.rem(place, array.shape[1]), 128)
        return array[:, pl.ds(start, width)]

    columns = jnp.concatenate([block_of(f) for f in features], axis=0)
    wide = out.shape[1] // groups
    for group in range(groups):
        own = grads[group * (count // 2) : (group + 1) * (count // 2)]
        rows = jnp.concatenate([g[...] for g in own], axis=0)
        cols = slice(group * wide, (group + 1) * wide)
        total = lax.dot_general(
            columns, rows, (((0,), (0,)), ((), ())), preferred_element_type=jnp.float32
        )
        for part in parts:
            total = total + part[:, cols].astype(jnp.float32)
        out[:, cols] = total.astype(out.dtype)


def dense_device(stash, scales, out_grad, route_ids, gates, w_gate_up, w_down):
    bf16, f32 = jnp.bfloat16, jnp.float32
    tokens, features_total = stash.shape
    width, hidden = w_down.shape[1:]
    double = 2 * hidden
    dp_count = lax.axis_size("dp")
    deep = dp_count // 4
    segment, half = 2 * width, features_total // 2

    def over_dp(value, bit):
        return lax.ppermute(value, "dp", [(i, i ^ bit) for i in range(dp_count)])

    def over_expert(value):
        return lax.ppermute(value, "expert", [(0, 1), (1, 0)])

    def after(value, *others):
        return lax.optimization_barrier((value, *others))[0]

    piece = w_down[0]
    other_piece = over_expert(piece)
    bits = [1 << b for b in reversed(range(deep.bit_length() - 1))]
    pieces = []
    for own in (piece, other_piece):
        held = {0: own}
        for bit in bits:
            held.update({r | bit: over_dp(p, 4 * bit) for r, p in held.items()})
        relatives = [4 * r for r in held]
        held = list(held.values())
        pieces.append(held + [over_dp(p, 1) for p in held])
    relatives = relatives + [r + 1 for r in relatives]

    sent_grad = pl.pallas_call(
        functools.partial(far_columns, segment),
        in_specs=[pl.BlockSpec(memory_space=pltpu.HBM)],
        out_specs=pl.BlockSpec(memory_space=pltpu.VMEM),
        out_shape=shaped((tokens, half), bf16),
        scratch_shapes=[pltpu.SemaphoreType.DMA((deep,))],
        compiler_params=pltpu.CompilerParams(vmem_limit_bytes=KERNEL_BYTES),
    )(out_grad)
    own_gate, other_gate = call(
        prepare_gates,
        (gates.T, after(route_ids.T, sent_grad)),
        (shaped((tokens, 128), f32), shaped((8, tokens), f32)),
    )
    got_gate = over_expert(other_gate)
    near, opposite, *same = call(
        functools.partial(dequantize_split, segment),
        (after(stash, sent_grad), scales.T),
        (
            shaped((tokens, half), bf16),
            shaped((tokens, half // 2), bf16),
            *(shaped((tokens, segment), bf16),) * (deep // 2),
        ),
    )
    weight_in = after(w_gate_up[0], near)
    got_opposite = over_expert(opposite)
    got_same = [over_expert(f) for f in same]
    got_near = over_expert(near)
    across_grad = over_dp(sent_grad, 2)
    across_opposite = over_dp(opposite, 2)
    across_got = over_dp(got_opposite, 2)
    across_same = [over_dp(f, 2) for f in same[1:]]
    across_got_same = [over_dp(f, 2) for f in got_same[1:]]

    up_cost = tokens * features_total * double
    (own_up,) = call(
        functools.partial(up_own, segment),
        (near, weight_in, opposite, *same),
        (shaped((tokens, double), f32),),
        2 * up_cost,
    )
    (got_up,) = call(
        functools.partial(up_far, segment),
        (weight_in, got_opposite, *got_same),
        (shaped((tokens, double), f32),),
        up_cost,
    )
    flops = 4 * tokens * half * hidden
    sums = shaped((tokens, hidden), bf16)
    kept, passed = call(
        functools.partial(hidden_mine, width, relatives),
        (out_grad, across_grad, *pieces[0]),
        (shaped((tokens, hidden), f32), sums),
        flops,
    )
    across_hidden = over_dp(passed, 2)
    direct, diagonal = call(
        functools.partial(hidden_other, width, relatives),
        (out_grad, across_grad, *pieces[1]),
        (sums, sums),
        flops,
    )
    got_direct = over_expert(direct)
    got_diagonal = lax.ppermute(
        diagonal,
        ("dp", "expert"),
        [(2 * i + y, 2 * (i ^ 2) + 1 - y) for i in range(dp_count) for y in range(2)],
    )
    grad_gate, grad_up = call(
        functools.partial(gated_body, segment),
        (got_near, weight_in, own_up, got_up, kept, across_hidden, got_direct, got_diagonal, own_gate, got_gate),
        (shaped((2 * tokens, hidden), bf16),) * 2,
        up_cost,
    )

    grads = []
    for own in (grad_gate, grad_up):
        across = over_dp(own, 2)
        grads.append([own, across, over_dp(own, 1), over_dp(across, 1)])

    def with_core(arrays):
        return arrays + [over_dp(a, 1) for a in arrays]

    shared_near = with_core([near, got_near])
    shared_self = with_core([same[0], got_same[0]])
    shared_far = with_core([across_opposite, across_got])
    shared_same = [with_core(list(pair)) for pair in zip(across_same, across_got_same)]

    returned, own_slots = [], []
    quarter = half // 2
    eighth = quarter // 2
    parts = ((0, quarter), (quarter, half + eighth), (half + quarter + eighth, eighth))
    for first_col, part_cols in parts:
        (sent_slots,) = call(
            functools.partial(slot_grads, tokens, first_col),
            (grad_gate, grad_up, weight_in),
            (shaped((tokens, part_cols), bf16),),
            up_cost,
        )
        returned.append(over_expert(sent_slots))
        (slots,) = call(
            functools.partial(slot_grads, 0, first_col),
            (grad_gate, grad_up, weight_in),
            (shaped((tokens, part_cols), bf16),),
            up_cost,
        )
        own_slots.append(slots)

    def block(relative, features, chosen, parts, dtype=bf16):
        wide = hidden * 2 * len(chosen) // len(features)
        (out,) = call(
            functools.partial(weight_block, len(features), width, relative),
            (*features, *chosen, *parts),
            (shaped((width, wide), dtype),),
            2 * len(features) * tokens * width * wide,
        )
        return out

    top = deep // 2
    dual = [g[n] for g in grads for n in (0, 2)]
    across = over_dp(block(0, shared_self, dual, ()), 2)
    wholes, last_parts = [], [[], []]
    arrived = {(r, g): [] for r in range(deep) for g in range(2)}
    for r in sorted(range(1, deep), key=lambda r: (r & -r, -r)):
        bit = r & -r
        far = shared_far if r >= top else shared_same[r - 1]
        quad = shared_near[:2] + far[:2] + shared_near[2:] + far[2:]
        if r == 1:
            wholes.append(over_dp(block(r, quad, grads[0] + grads[1], ()), 4 * bit))
            continue
        for g in range(2):
            total = block(r, quad, grads[g], arrived[r, g])
            moved = over_dp(total, 4 * bit)
            (arrived[r ^ bit, g] if r != bit else last_parts[g]).append(moved)
    ready = block(0, shared_near, dual, (across,), f32)
    sums = (ready, *wholes, *[p for pair in zip(*last_parts) for p in pair])
    grad = pl.pallas_call(
        functools.partial(weight_last, 1.0 / dp_count, len(wholes)),
        in_specs=[pl.BlockSpec(memory_space=pltpu.VMEM) for _ in sums],
        out_specs=pl.BlockSpec(memory_space=pl.ANY),
        out_shape=shaped((width, double), f32),
        scratch_shapes=[pltpu.VMEM((2, width, hidden), f32), pltpu.SemaphoreType.DMA((2,))],
        compiler_params=pltpu.CompilerParams(vmem_limit_bytes=KERNEL_BYTES),
    )(*sums)
    input_grad = None
    for order, (first_col, part_cols) in enumerate(parts):
        input_grad = fill_columns(
            functools.partial(combine_columns, first_col),
            (own_slots[order], returned[order]),
            shaped(stash.shape, bf16),
            part_cols,
            input_grad,
        )
    return input_grad, grad[None]


def solution(mesh):
    dp_count, experts = mesh.shape["dp"], mesh.shape["expert"]
    power = dp_count >= 16 and dp_count & (dp_count - 1) == 0

    def program(stash, scales, out_grad, route_ids, *rest):
        if not (experts == route_ids.shape[1] == 2 and power):
            return on_device(stash, scales, out_grad, route_ids, *rest)
        return dense_device(stash, scales, out_grad, route_ids, *rest)

    placed = (
        P(("dp", "expert"), None),
        P(("dp", "expert"), None),
        P(("dp", "expert"), None),
        P(("dp", "expert"), None),
        P(("dp", "expert"), None),
        P("expert", None, None),
        P("expert", "dp", None),
    )
    return jax.shard_map(
        program,
        mesh=mesh,
        in_specs=placed,
        out_specs=(P(("dp", "expert"), None), P("expert", "dp", None)),
        check_vma=False,
    )
```

```python
import functools
import math

import jax
import jax.numpy as jnp
from jax import lax
from jax.experimental import pallas as pl
from jax.experimental.pallas import tpu as pltpu
from jax.sharding import PartitionSpec as P


KERNEL_BYTES = 16 << 20


def dispatch_plan(route_ids, experts, capacity, tokens):
    flat_ids = route_ids.reshape(-1)
    onehot = (flat_ids[:, None] == jnp.arange(experts, dtype=jnp.int32)[None, :]).astype(jnp.int32)
    earlier = jnp.cumsum(onehot, axis=0) - onehot
    ranking = jnp.sum(earlier * onehot, axis=1)
    destination = flat_ids * capacity + ranking
    slot_total = 2 * tokens
    source = jnp.full((experts * capacity,), slot_total, jnp.int32)
    source = source.at[destination].set(jnp.arange(slot_total, dtype=jnp.int32))
    return (destination, source)


def dequantize(stash_rows, scale_rows):
    row_total = stash_rows.shape[0]
    blocks = scale_rows.shape[1]
    scaled = (
        stash_rows.reshape(row_total, blocks, -1).astype(jnp.float32)
        * scale_rows.astype(jnp.float32)[:, :, None]
    )
    return scaled.reshape(row_total, -1).astype(jnp.bfloat16)


def gated_backward(gate_up, back_hidden):
    hidden = back_hidden.shape[1]
    gate_value = gate_up[:, :hidden]
    up_value = gate_up[:, hidden:]
    sigmoid_gate = jax.nn.sigmoid(gate_value)
    grad_gate = back_hidden * up_value * sigmoid_gate * (1.0 + gate_value * (1.0 - sigmoid_gate))
    grad_up = back_hidden * gate_value * sigmoid_gate
    return jnp.concatenate([grad_gate, grad_up], axis=1).astype(jnp.bfloat16)


def on_device(stash, scales, out_grad, route_ids, gates, w_gate_up, w_down):
    tokens, feature_width = stash.shape
    blocks = scales.shape[1]
    hidden = w_down.shape[2]
    experts = lax.axis_size("expert")
    dp_count = lax.axis_size("dp")
    capacity = min(tokens, 7 * tokens // (2 * experts))
    row_total = experts * capacity
    destination, source = dispatch_plan(route_ids, experts, capacity, tokens)
    slot_total = 2 * tokens
    live_rows = (source < slot_total)[:, None]
    token_index = jnp.minimum(source // 2, tokens - 1)
    slot_index = jnp.minimum(source, slot_total - 1)
    sent_stash = jnp.where(live_rows, stash[token_index], jnp.zeros((), stash.dtype))
    sent_stash = sent_stash.reshape(experts, capacity, feature_width)
    sent_scale = jnp.where(live_rows, scales[token_index], jnp.zeros((), scales.dtype))
    sent_scale = sent_scale.reshape(experts, capacity, blocks)
    weighted = gates.reshape(-1)[slot_index][:, None] * out_grad[token_index].astype(jnp.float32)
    sent_grad = jnp.where(live_rows, weighted, jnp.zeros((), jnp.float32)).astype(jnp.bfloat16)
    sent_grad = sent_grad.reshape(experts, capacity, feature_width)
    weight_in = w_gate_up[0]
    got_stash, got_scale, got_grad = (
        lax.all_to_all(sent_stash, "expert", split_axis=0, concat_axis=0, tiled=True),
        lax.all_to_all(sent_scale, "expert", split_axis=0, concat_axis=0, tiled=True),
        lax.all_to_all(sent_grad, "expert", split_axis=0, concat_axis=0, tiled=True),
    )
    features = dequantize(
        got_stash.reshape(row_total, feature_width), got_scale.reshape(row_total, blocks)
    )
    gate_up = jnp.dot(features, weight_in, preferred_element_type=jnp.float32)
    upstream = got_grad.reshape(row_total, feature_width)
    back_hidden = jnp.dot(
        upstream,
        lax.all_gather(w_down, "dp", axis=1, tiled=True)[0],
        preferred_element_type=jnp.float32,
    )
    hidden_grad = gated_backward(gate_up, back_hidden)
    slot_grads = lax.dot_general(
        hidden_grad, weight_in, (((1,), (1,)), ((), ())), preferred_element_type=jnp.float32
    ).astype(jnp.bfloat16)
    returned = lax.all_to_all(
        slot_grads.reshape(experts, capacity, feature_width),
        "expert",
        split_axis=0,
        concat_axis=0,
        tiled=True,
    )
    picked = returned.reshape(row_total, feature_width)[destination].astype(jnp.float32)
    input_grad = jnp.sum(picked.reshape(tokens, 2, feature_width), axis=1).astype(jnp.bfloat16)
    local_rows = feature_width // dp_count
    summed = lax.psum_scatter(
        lax.dot_general(
            features, hidden_grad, (((0,), (0,)), ((), ())), preferred_element_type=jnp.float32
        ).astype(jnp.bfloat16),
        "dp",
        scatter_dimension=0,
        tiled=True,
    ).astype(jnp.float32)
    grad_gate_up = (summed / dp_count).reshape(1, local_rows, 2 * hidden)
    return (input_grad, grad_gate_up)


def call(body, ins, outs, flops=0):
    moved = sum(math.prod(a.shape) * jnp.dtype(a.dtype).itemsize for a in (*ins, *outs))
    kept = pl.BlockSpec(memory_space=pltpu.VMEM)
    return pl.pallas_call(
        body,
        in_specs=[kept for _ in ins],
        out_specs=[kept for _ in outs],
        out_shape=outs,
        cost_estimate=pl.CostEstimate(flops=flops, bytes_accessed=moved, transcendentals=0),
        compiler_params=pltpu.CompilerParams(vmem_limit_bytes=KERNEL_BYTES),
    )(*ins)


def fill_columns(body, ins, out, wide, filled):
    kept, away = pl.BlockSpec(memory_space=pltpu.VMEM), pl.BlockSpec(memory_space=pl.ANY)
    more = () if filled is None else (filled,)
    return pl.pallas_call(
        body,
        in_specs=[kept for _ in ins] + [away for _ in more],
        out_specs=away,
        out_shape=out,
        scratch_shapes=[pltpu.VMEM((out.shape[0], wide), out.dtype), pltpu.SemaphoreType.DMA],
        input_output_aliases={len(ins): 0} if more else {},
        compiler_params=pltpu.CompilerParams(vmem_limit_bytes=KERNEL_BYTES),
    )(*ins, *more)


def shaped(shape, dtype):
    return jax.ShapeDtypeStruct(shape, dtype)


def far_columns(segment, source, out, sem):
    far_side = 1 - lax.rem(lax.axis_index("dp") // 2, 2)
    copies = []
    for k in range(out.shape[1] // segment):
        start = pl.multiple_of((2 * k + far_side) * segment, 128)
        target = out.at[:, k * segment : (k + 1) * segment]
        copies.append(pltpu.make_async_copy(source.at[:, pl.ds(start, segment)], target, sem.at[k]))
        copies[k].start()
    for copy in copies:
        copy.wait()


def prepare_gates(gates, route_ids, own_gate, other_gate):
    first = route_ids[0:1, :] == lax.axis_index("expert")
    mine = jnp.where(first, gates[0:1, :], gates[1:2, :])
    theirs = jnp.where(first, gates[1:2, :], gates[0:1, :])
    own_gate[...] = jnp.transpose(jnp.broadcast_to(mine, (128, own_gate.shape[0])))
    other_gate[...] = jnp.broadcast_to(theirs, other_gate.shape)


def dequantize_split(segment, urgent, stash, scales, *outs):
    mine = lax.axis_index("dp")
    block = stash.shape[1] // scales.shape[0]
    deep = stash.shape[1] // (2 * segment)
    near, opposite, same = (None, outs[0], ()) if urgent else (outs[0], None, outs[1:])
    level = deep // 2
    columns = jnp.transpose(scales[...].astype(jnp.float32))

    def fill(x_here, z_here):
        for b in range(scales.shape[0]):
            chip, inside = divmod(b * block, segment)
            z, x = divmod(chip, 2)
            away = x != x_here and z ^ z_here >= level
            if away != urgent:
                continue
            scaled = stash[:, b * block : (b + 1) * block].astype(jnp.float32)
            scaled = (scaled * columns[:, b : b + 1]).astype(jnp.bfloat16)
            if away:
                target, start = opposite, z % level * segment
            elif x == x_here:
                target, start = near, z * segment
            else:
                target, start = same[z ^ z_here], 0
            target[:, start + inside : start + inside + block] = scaled

    for x_here in range(2):
        for z_here in range(deep):
            pl.when(mine // 2 == 2 * z_here + x_here)(functools.partial(fill, x_here, z_here))


def hidden_sums(width, relatives, out_grad, across, pieces):
    mine = lax.axis_index("dp")
    upper = lower = None
    for piece, relative in zip(pieces, relatives):
        block = mine ^ relative
        here = pl.multiple_of(block * width, 128)
        there = pl.multiple_of((2 * (block // 4) + lax.rem(block, 2)) * width, 128)
        weight = piece[...]
        one = jnp.dot(out_grad[:, pl.ds(here, width)], weight, preferred_element_type=jnp.float32)
        two = jnp.dot(across[:, pl.ds(there, width)], weight, preferred_element_type=jnp.float32)
        upper = one if upper is None else upper + one
        lower = two if lower is None else lower + two
    return upper, lower


def hidden_mine(width, relatives, out_grad, across, *refs):
    kept, passed = refs[-2:]
    kept[...], lower = hidden_sums(width, relatives, out_grad, across, refs[:-2])
    passed[...] = lower.astype(jnp.bfloat16)


def hidden_other(width, relatives, out_grad, across, *refs):
    direct, diagonal = refs[-2:]
    upper, lower = hidden_sums(width, relatives, out_grad, across, refs[:-2])
    direct[...] = upper.astype(jnp.bfloat16)
    diagonal[...] = lower.astype(jnp.bfloat16)


def feature_product(segment, features, weight_in, x_offset, base):
    side = lax.rem(lax.axis_index("dp") // 2 + x_offset, 2)
    total = None
    for k in range(features.shape[1] // segment):
        rows = pl.multiple_of((2 * (base + k) + side) * segment, 128)
        term = jnp.dot(
            features[:, k * segment : (k + 1) * segment],
            weight_in[pl.ds(rows, segment), :],
            preferred_element_type=jnp.float32,
        )
        total = term if total is None else total + term
    return total


def up_far(segment, weight_in, opposite, *refs):
    same, out = refs[:-1], refs[-1]
    z = lax.axis_index("dp") // 4
    total = feature_product(segment, opposite, weight_in, 1, len(same) - z // len(same) * len(same))
    for r, features in enumerate(same):
        total += feature_product(segment, features, weight_in, 1, z ^ r)
    out[...] = total


def up_own(segment, near, weight_in, *refs):
    up_far(segment, weight_in, *refs)
    refs[-1][...] += feature_product(segment, near, weight_in, 0, 0)


def gated_body(
    segment, near, weight_in, own_up, got_up, kept, across, direct, diagonal, own_gate, got_gate, out_gate, out_up
):
    tokens, double = own_up.shape
    hidden = double // 2
    own_back = (kept[...] + across[...].astype(jnp.float32)) * own_gate[:, 0:1]
    gates = jnp.transpose(jnp.broadcast_to(got_gate[0:1, :], (128, tokens)))
    got_back = (direct[...].astype(jnp.float32) + diagonal[...].astype(jnp.float32)) * gates[:, 0:1]
    others = got_up[...] + feature_product(segment, near, weight_in, 0, 0)
    for half, (gate_up, back) in enumerate(((own_up[...], own_back), (others, got_back))):
        rows = slice(half * tokens, (half + 1) * tokens)
        gate, up = gate_up[:, :hidden], gate_up[:, hidden:]
        sig = jax.nn.sigmoid(gate)
        out_gate[rows] = (back * up * sig * (1.0 + gate * (1.0 - sig))).astype(jnp.bfloat16)
        out_up[rows] = (back * gate * sig).astype(jnp.bfloat16)


def write_columns(start, out, rows, held, sem):
    held[...] = rows.astype(held.dtype)
    copy = pltpu.make_async_copy(held, out.at[:, pl.ds(start, held.shape[1])], sem)
    copy.start()
    copy.wait()


def combine_columns(start, own, got, *refs):
    write_columns(start, *refs[-3:-2], own[...].astype(jnp.float32) + got[...].astype(jnp.float32), *refs[-2:])


def weight_last(scale, wholes, ready, *refs):
    parts, out, held, sem = refs[:-3], *refs[-3:]
    wide = out.shape[1] // 2
    copies = []
    for group in range(2):
        cols = slice(group * wide, (group + 1) * wide)
        total = ready[:, cols]
        for part in parts[:wholes]:
            total = total + part[:, cols].astype(jnp.float32)
        for part in parts[wholes + group :: 2]:
            total = total + part[...].astype(jnp.float32)
        held[group] = total * scale
        copies.append(pltpu.make_async_copy(held.at[group], out.at[:, cols], sem.at[group]))
        copies[group].start()
    for copy in copies:
        copy.wait()


def slot_grads(first_row, first_col, grad_gate, grad_up, weight_in, out):
    tokens, total = out.shape
    hidden = grad_gate.shape[1]
    rows = slice(first_row, first_row + tokens)
    step = math.gcd(total, 512)
    for start in range(0, total, step):
        cols = slice(start, start + step)
        weight = weight_in[first_col + start : first_col + start + step]
        value = sum(
            lax.dot_general(g[rows], w, (((1,), (1,)), ((), ())), preferred_element_type=jnp.float32)
            for g, w in ((grad_gate, weight[:, :hidden]), (grad_up, weight[:, hidden:]))
        )
        out[:, cols] = value.astype(jnp.bfloat16)


def weight_block(count, width, relative, *refs):
    features, out = refs[:count], refs[-1]
    groups = out.shape[1] // refs[count].shape[1]
    grads, parts = refs[count : count + groups * (count // 2)], refs[count + groups * (count // 2) : -1]
    mine = lax.axis_index("dp")
    place = (2 * ((mine // 4) ^ relative) + lax.rem(mine, 2)) * width

    def block_of(array):
        start = pl.multiple_of(lax.rem(place, array.shape[1]), 128)
        return array[:, pl.ds(start, width)]

    columns = jnp.concatenate([block_of(f) for f in features], axis=0)
    wide = out.shape[1] // groups
    for group in range(groups):
        own = grads[group * (count // 2) : (group + 1) * (count // 2)]
        rows = jnp.concatenate([g[...] for g in own], axis=0)
        cols = slice(group * wide, (group + 1) * wide)
        total = lax.dot_general(
            columns, rows, (((0,), (0,)), ((), ())), preferred_element_type=jnp.float32
        )
        for part in parts:
            total = total + part[:, cols].astype(jnp.float32)
        out[:, cols] = total.astype(out.dtype)


def dense_device(stash, scales, out_grad, route_ids, gates, w_gate_up, w_down):
    bf16, f32 = jnp.bfloat16, jnp.float32
    tokens, features_total = stash.shape
    width, hidden = w_down.shape[1:]
    double = 2 * hidden
    dp_count = lax.axis_size("dp")
    deep = dp_count // 4
    segment, half = 2 * width, features_total // 2

    def over_dp(value, bit):
        return lax.ppermute(value, "dp", [(i, i ^ bit) for i in range(dp_count)])

    def over_expert(value):
        return lax.ppermute(value, "expert", [(0, 1), (1, 0)])

    def after(value, *others):
        return lax.optimization_barrier((value, *others))[0]

    piece = w_down[0]
    other_piece = over_expert(piece)
    bits = [1 << b for b in reversed(range(deep.bit_length() - 1))]
    pieces = []
    for own in (piece, other_piece):
        held = {0: own}
        for bit in bits:
            held.update({r | bit: over_dp(p, 4 * bit) for r, p in held.items()})
        relatives = [4 * r for r in held]
        held = list(held.values())
        pieces.append(held + [over_dp(p, 1) for p in held])
    relatives = relatives + [r + 1 for r in relatives]

    sent_grad = pl.pallas_call(
        functools.partial(far_columns, segment),
        in_specs=[pl.BlockSpec(memory_space=pltpu.HBM)],
        out_specs=pl.BlockSpec(memory_space=pltpu.VMEM),
        out_shape=shaped((tokens, half), bf16),
        scratch_shapes=[pltpu.SemaphoreType.DMA((deep,))],
        compiler_params=pltpu.CompilerParams(vmem_limit_bytes=KERNEL_BYTES),
    )(out_grad)
    own_gate, other_gate = call(
        prepare_gates,
        (gates.T, after(route_ids.T, sent_grad)),
        (shaped((tokens, 128), f32), shaped((8, tokens), f32)),
    )
    got_gate = over_expert(other_gate)
    (opposite,) = call(
        functools.partial(dequantize_split, segment, True),
        (after(stash, sent_grad), scales.T),
        (shaped((tokens, half // 2), bf16),),
    )
    near, *same = call(
        functools.partial(dequantize_split, segment, False),
        (after(stash, opposite), scales.T),
        (shaped((tokens, half), bf16), *(shaped((tokens, segment), bf16),) * (deep // 2)),
    )
    weight_in = after(w_gate_up[0], near)
    got_opposite = over_expert(opposite)
    got_same = [over_expert(f) for f in same]
    got_near = over_expert(near)
    across_grad = over_dp(sent_grad, 2)
    across_opposite = over_dp(opposite, 2)
    across_got = over_dp(got_opposite, 2)
    across_same = [over_dp(f, 2) for f in same[1:]]
    across_got_same = [over_dp(f, 2) for f in got_same[1:]]

    up_cost = tokens * features_total * double
    (own_up,) = call(
        functools.partial(up_own, segment),
        (near, weight_in, opposite, *same),
        (shaped((tokens, double), f32),),
        2 * up_cost,
    )
    (got_up,) = call(
        functools.partial(up_far, segment),
        (weight_in, got_opposite, *got_same),
        (shaped((tokens, double), f32),),
        up_cost,
    )
    flops = 4 * tokens * half * hidden
    sums = shaped((tokens, hidden), bf16)
    kept, passed = call(
        functools.partial(hidden_mine, width, relatives),
        (out_grad, across_grad, *pieces[0]),
        (shaped((tokens, hidden), f32), sums),
        flops,
    )
    across_hidden = over_dp(passed, 2)
    direct, diagonal = call(
        functools.partial(hidden_other, width, relatives),
        (out_grad, across_grad, *pieces[1]),
        (sums, sums),
        flops,
    )
    got_direct = over_expert(direct)
    got_diagonal = lax.ppermute(
        diagonal,
        ("dp", "expert"),
        [(2 * i + y, 2 * (i ^ 2) + 1 - y) for i in range(dp_count) for y in range(2)],
    )
    grad_gate, grad_up = call(
        functools.partial(gated_body, segment),
        (got_near, weight_in, own_up, got_up, kept, across_hidden, got_direct, got_diagonal, own_gate, got_gate),
        (shaped((2 * tokens, hidden), bf16),) * 2,
        up_cost,
    )

    grads = []
    for own in (grad_gate, grad_up):
        across = over_dp(own, 2)
        grads.append([own, across, over_dp(own, 1), over_dp(across, 1)])

    def with_core(arrays):
        return arrays + [over_dp(a, 1) for a in arrays]

    shared_near = with_core([near, got_near])
    shared_self = with_core([same[0], got_same[0]])
    shared_far = with_core([across_opposite, across_got])
    shared_same = [with_core(list(pair)) for pair in zip(across_same, across_got_same)]

    returned, own_slots = [], []
    quarter = half // 2
    eighth = quarter // 2
    parts = ((0, quarter), (quarter, half + eighth), (half + quarter + eighth, eighth))
    for first_col, part_cols in parts:
        (sent_slots,) = call(
            functools.partial(slot_grads, tokens, first_col),
            (grad_gate, grad_up, weight_in),
            (shaped((tokens, part_cols), bf16),),
            up_cost,
        )
        returned.append(over_expert(sent_slots))
        (slots,) = call(
            functools.partial(slot_grads, 0, first_col),
            (grad_gate, grad_up, weight_in),
            (shaped((tokens, part_cols), bf16),),
            up_cost,
        )
        own_slots.append(slots)

    def block(relative, features, chosen, parts, dtype=bf16):
        wide = hidden * 2 * len(chosen) // len(features)
        (out,) = call(
            functools.partial(weight_block, len(features), width, relative),
            (*features, *chosen, *parts),
            (shaped((width, wide), dtype),),
            2 * len(features) * tokens * width * wide,
        )
        return out

    top = deep // 2
    dual = [g[n] for g in grads for n in (0, 2)]
    across = over_dp(block(0, shared_self, dual, ()), 2)
    wholes, last_parts = [], [[], []]
    arrived = {(r, g): [] for r in range(deep) for g in range(2)}
    for r in sorted(range(1, deep), key=lambda r: (r & -r, -r)):
        bit = r & -r
        far = shared_far if r >= top else shared_same[r - 1]
        quad = shared_near[:2] + far[:2] + shared_near[2:] + far[2:]
        if r == 1:
            wholes.append(over_dp(block(r, quad, grads[0] + grads[1], ()), 4 * bit))
            continue
        for g in range(2):
            total = block(r, quad, grads[g], arrived[r, g])
            moved = over_dp(total, 4 * bit)
            (arrived[r ^ bit, g] if r != bit else last_parts[g]).append(moved)
    ready = block(0, shared_near, dual, (across,), f32)
    sums = (ready, *wholes, *[p for pair in zip(*last_parts) for p in pair])
    grad = pl.pallas_call(
        functools.partial(weight_last, 1.0 / dp_count, len(wholes)),
        in_specs=[pl.BlockSpec(memory_space=pltpu.VMEM) for _ in sums],
        out_specs=pl.BlockSpec(memory_space=pl.ANY),
        out_shape=shaped((width, double), f32),
        scratch_shapes=[pltpu.VMEM((2, width, hidden), f32), pltpu.SemaphoreType.DMA((2,))],
        compiler_params=pltpu.CompilerParams(vmem_limit_bytes=KERNEL_BYTES),
    )(*sums)
    input_grad = None
    for order, (first_col, part_cols) in enumerate(parts):
        input_grad = fill_columns(
            functools.partial(combine_columns, first_col),
            (own_slots[order], returned[order]),
            shaped(stash.shape, bf16),
            part_cols,
            input_grad,
        )
    return input_grad, grad[None]


def solution(mesh):
    dp_count, experts = mesh.shape["dp"], mesh.shape["expert"]
    power = dp_count >= 16 and dp_count & (dp_count - 1) == 0

    def program(stash, scales, out_grad, route_ids, *rest):
        if not (experts == route_ids.shape[1] == 2 and power):
            return on_device(stash, scales, out_grad, route_ids, *rest)
        return dense_device(stash, scales, out_grad, route_ids, *rest)

    placed = (
        P(("dp", "expert"), None),
        P(("dp", "expert"), None),
        P(("dp", "expert"), None),
        P(("dp", "expert"), None),
        P(("dp", "expert"), None),
        P("expert", None, None),
        P("expert", "dp", None),
    )
    return jax.shard_map(
        program,
        mesh=mesh,
        in_specs=placed,
        out_specs=(P(("dp", "expert"), None), P("expert", "dp", None)),
        check_vma=False,
    )
```
